32 devices in a mesh: gx: 16 (over z, y, x), gy: 2 (over core).
Axes of the slice: x: 2, y: 2, z: 4, core: 2. Of those that a mesh axis runs over, the one named last changes fastest.
Arguments:
- observed: float32 [8192, 128], P(('gx', 'gy')), may hold values from -6 to 6
- jacobian: bfloat16 [8192, 64, 128], P(('gx', 'gy'))
- tile_block: int32 [8192], P(('gx', 'gy')), may hold values from 0 to 127
- params: float32 [128, 64], replicated, may hold values from -3 to 3
- damping: float32 [1], replicated, may hold values from 0.05 to 2
Outputs:
- scaled_step: float32 [128, 64], P('gy')
- misfit: float32 [], replicated
The draws below stay inside these ranges and needn't reach their ends.
All inputs are finite; a program needn't handle non-finite values.
Results may differ from the reference program's by a relative error of at most 0.0031.
Values sent between devices are 32-bit elements; how exact they have to be, the bound alone decides.
No kernel may reach another device: no remote copies, remote signals or barrier semaphores. Data moves between devices by JAX's collectives and lax.ppermute only.
A program may use at most 64 MiB of HBM per device.

```python
import math
import jax
import jax.numpy as jnp
from jax import lax

VOX = 128
BLK = 64
NB = 128
TILES_PER_UNIT = 256
TILES = 8192
DEVICES = 32


def shared_blocks(key):
    return jax.random.randint(jax.random.fold_in(key, 11), (TILES,), 0, NB, dtype=jnp.int32)


def draw_tile_block(key, part):
    return shared_blocks(key)


def draw_jacobian(key, part):
    blocks = shared_blocks(key)
    mix_key = jax.random.fold_in(key, 23)
    scale_key = jax.random.fold_in(key, 37)
    noise_key = jax.random.fold_in(key, 41)
    reach = 7
    lowest = 0.3
    highest = 3.0
    coupling = jax.random.randint(mix_key, (NB, BLK, BLK), -1, 2, dtype=jnp.int32).astype(jnp.float32)
    mixing = coupling + 10.0 * jnp.eye(BLK, dtype=jnp.float32)[None]
    row_scale = jnp.exp(jax.random.uniform(scale_key, (NB, BLK), jnp.float32, math.log(lowest), math.log(highest)))
    noise_var = reach * (reach + 1) / 3.0
    norm_factor = 1.0 / math.sqrt(VOX * noise_var * (100.0 + 2.0 * BLK / 3.0))
    factor = row_scale * norm_factor
    group_count = TILES // TILES_PER_UNIT
    grouped = blocks.reshape(group_count, TILES_PER_UNIT)

    def one_group(index):
        ids = grouped[index]
        noise = jax.random.randint(jax.random.fold_in(noise_key, index), (TILES_PER_UNIT, BLK, VOX), -reach, reach + 1, dtype=jnp.int32).astype(jnp.float32)
        chosen = mixing[ids]
        mixed = jnp.einsum('tpq,tqv->tpv', chosen, noise, precision=lax.Precision.HIGHEST)
        return (mixed * factor[ids][:, :, None]).astype(jnp.bfloat16)
    stacked = lax.map(one_group, jnp.arange(group_count, dtype=jnp.int32))
    return stacked.reshape(TILES, BLK, VOX)


def block_levels(stream_key, shape, shards, low, top_value):
    level, own = 1.0, jax.random.fold_in(stream_key, 6)
    for axis_at, parts in shards:
        heights = jnp.exp(jax.random.uniform(jax.random.fold_in(own, axis_at), (parts,), jnp.float32, low / len(shards), top_value / len(shards)))
        level = level * jnp.repeat(heights, shape[axis_at] // parts).reshape([-1 if axis == axis_at else 1 for axis in range(len(shape))])
    return level


def bell_draw(own_key, shape, width, bound, split=(), kind=jnp.bfloat16):
    array = width * jax.random.normal(own_key, shape, jnp.float32)
    if split:
        array = array * block_levels(own_key, shape, split, -0.22, 0.18)
    return jnp.clip(array, -bound, bound).astype(kind)


def setup_inputs(seed: int = 0) -> dict:
    seeds = jax.random.split(jax.random.key(seed), 6)
    observed = bell_draw(seeds[0], (TILES, VOX), 1.0, 6.0, ((0, 32),), jnp.float32)
    jacobian = draw_jacobian(jax.random.fold_in(seeds[5], 71), 0)
    tile_block = draw_tile_block(jax.random.fold_in(seeds[5], 71), 0)
    params = bell_draw(seeds[3], (NB, BLK), 0.5, 3.0, (), jnp.float32)
    damping = jnp.clip(jnp.exp(jax.random.uniform(seeds[4], (1,), jnp.float32, math.log(0.05), math.log(2.0))), 0.05, 2.0)
    return dict(observed=observed, jacobian=jacobian, tile_block=tile_block, params=params, damping=damping)


def solve_blocks(system, rhs):
    size = system.shape[1]
    augmented = jnp.concatenate([system, rhs[:, :, None]], axis=2)
    augmented = jnp.transpose(augmented, (1, 2, 0))
    row_ids = jnp.arange(size, dtype=jnp.int32)

    def eliminate(step, current):
        column = step.astype(jnp.int32)
        pivot_row = lax.dynamic_index_in_dim(current, column, 0, keepdims=False)
        pivot = lax.dynamic_index_in_dim(pivot_row, column, 0, keepdims=False)
        pivot_row = pivot_row / pivot[None, :]
        factors = lax.dynamic_index_in_dim(current, column, 1, keepdims=False)
        updated = current - factors[:, None, :] * pivot_row[None, :, :]
        is_pivot = (row_ids == column)[:, None, None]
        return jnp.where(is_pivot, pivot_row[None, :, :], updated)
    final = lax.fori_loop(0, size, eliminate, augmented)
    return jnp.transpose(final[:, size, :], (1, 0))

def reference(observed, jacobian, tile_block, params, damping):
    reflected_values = observed[::-1, ::-1]
    block_ids = jnp.arange(NB, dtype=jnp.int32)

    def partial_sums(carry, index):
        gram, grad, misfit = carry
        leading_entry = (index * TILES_PER_UNIT).astype(jnp.int32)
        measured_portion = lax.dynamic_slice_in_dim(observed, leading_entry, TILES_PER_UNIT, 0)
        reflected_portion = lax.dynamic_slice_in_dim(reflected_values, leading_entry, TILES_PER_UNIT, 0)
        jac_part = lax.dynamic_slice_in_dim(jacobian, leading_entry, TILES_PER_UNIT, 0).astype(jnp.float32)
        blk_part = lax.dynamic_slice_in_dim(tile_block, leading_entry, TILES_PER_UNIT, 0)
        onehot = (blk_part[:, None] == block_ids[None, :]).astype(jnp.float32)
        tile_params = jnp.dot(onehot, params, precision=lax.Precision.HIGHEST).astype(jnp.bfloat16)
        calculated_values = jnp.einsum('tpv,tp->tv', jac_part, tile_params.astype(jnp.float32))
        residual_values = 0.5 * (measured_portion + reflected_portion) - calculated_values
        misfit = misfit + jnp.sum(residual_values * residual_values)
        resid_b = residual_values.astype(jnp.bfloat16).astype(jnp.float32)
        tile_grad = jnp.einsum('tpv,tv->tp', jac_part, resid_b)
        tile_gram = jnp.einsum('tpv,tqv->tpq', jac_part, jac_part)
        gram = gram + jnp.einsum('tb,tpq->bpq', onehot, tile_gram, precision=lax.Precision.HIGHEST)
        grad = grad + jnp.dot(onehot.T, tile_grad, precision=lax.Precision.HIGHEST)
        return ((gram, grad, misfit), None)
    start = (jnp.zeros((NB, BLK, BLK), jnp.float32), jnp.zeros((NB, BLK), jnp.float32), jnp.zeros((), jnp.float32))
    (gram, grad, misfit), _ = lax.scan(partial_sums, start, jnp.arange(DEVICES, dtype=jnp.int32))
    misfit = misfit / (TILES * VOX)
    diagonal = jnp.diagonal(gram, axis1=1, axis2=2)
    eye = jnp.eye(BLK, dtype=jnp.float32)
    system = gram + damping[0] * diagonal[:, :, None] * eye[None] + eye[None]
    delta = solve_blocks(system, grad)
    return (delta * jnp.sqrt(diagonal), misfit)
```

```python
import jax
import jax.numpy as jnp
from jax import lax
from jax.experimental import pallas as pl
from jax.experimental.pallas import tpu as pltpu
from jax.sharding import PartitionSpec as P

NB = 128
STEP_TILES = 32
GROUP = 8
EXTRA = 8


def flipped(value, axes, size):
    return lax.ppermute(value, axes, [(i, size - 1 - i) for i in range(size)])


def xored(value, axis, bit):
    return lax.ppermute(value, axis, [(i, i ^ bit) for i in range(lax.axis_size(axis))])


def nt_dot(a, b):
    return lax.dot_general(a, b, (((1,), (1,)), ((), ())), preferred_element_type=jnp.float32)


def gram_body(tb, where_, j_ref, par_ref, calc_ref, keep_ref, send_ref, diag_ref, acc):
    step = pl.program_id(0)
    blk = j_ref.shape[1]
    half = blk // 2

    @pl.when(step == 0)
    def _():
        acc[...] = jnp.zeros_like(acc)

    def group(g, carry):
        base = g * GROUP
        rows = []
        grams = []
        for u in range(GROUP):
            b = tb[step * STEP_TILES + base + u]
            jac = j_ref[base + u]
            grams.append((b, nt_dot(jac, jac)))
            par = par_ref[pl.ds(b, 1), :].astype(jnp.bfloat16)
            rows.append(jnp.dot(par, jac, preferred_element_type=jnp.float32))
        calc_ref[pl.ds(pl.multiple_of(base, GROUP), GROUP), :] = jnp.concatenate(rows, axis=0)
        for b, gram in grams:
            acc[b] += gram
        return carry

    lax.fori_loop(0, STEP_TILES // GROUP, group, 0)

    @pl.when(step == pl.num_programs(0) - 1)
    def _():
        chunks = keep_ref.shape[0]
        pairs = (keep_ref.shape[1] - EXTRA) // half
        row = lax.broadcasted_iota(jnp.int32, (half, 2 * blk), 0)
        lane = lax.broadcasted_iota(jnp.int32, (half, 2 * blk), 1) % blk
        use_bot = (lane < half) & (row > lane)
        frow = lax.broadcasted_iota(jnp.int32, (blk, 2 * blk), 0)
        flane = lax.broadcasted_iota(jnp.int32, (blk, 2 * blk), 1) % blk
        on_diag = frow == flane

        for part, ref in enumerate((keep_ref, send_ref)):
            def chunk(c, carry, part=part, ref=ref):
                first = where_[part * chunks + c]
                for p in range(pairs):
                    full = jnp.concatenate([acc[first + 2 * p], acc[first + 2 * p + 1]], axis=1)
                    bot = pltpu.roll(full[half:], 2 * blk - half, 1)
                    ref[c, p * half : (p + 1) * half, :] = jnp.where(use_bot, bot, full[:half])
                    diag_ref[part, c, p : p + 1, :] = jnp.sum(
                        jnp.where(on_diag, full, 0.0), axis=0, keepdims=True
                    )
                return carry

            lax.fori_loop(0, chunks, chunk, 0)


def grad_body(tb, where_, j_ref, calc_ref, obs_ref, mir_ref, diag_ref, keep_in, send_in, keep_ref, send_ref, gacc, mis):
    step = pl.program_id(0)

    @pl.when(step == 0)
    def _():
        gacc[...] = jnp.zeros_like(gacc)
        mis[...] = jnp.zeros_like(mis)

    def group(g, carry):
        base = pl.multiple_of(g * GROUP, GROUP)
        rows = pl.ds(base, GROUP)
        resid = 0.5 * (obs_ref[rows, :] + mir_ref[rows, :]) - calc_ref[rows, :]
        mis[...] += resid * resid
        resid_b = resid.astype(jnp.bfloat16)
        grads = []
        for u in range(GROUP):
            grads.append(nt_dot(resid_b, j_ref[base + u])[u : u + 1, :])
        for u in range(GROUP):
            b = tb[step * STEP_TILES + base + u]
            gacc[pl.ds(b, 1), :] += grads[u]
        return carry

    lax.fori_loop(0, STEP_TILES // GROUP, group, 0)

    @pl.when(step == pl.num_programs(0) - 1)
    def _():
        chunks = keep_ref.shape[0]
        pairs = diag_ref.shape[2]
        total = jnp.sum(mis[...], axis=0, keepdims=True)
        rest = jnp.zeros((EXTRA - 2 * pairs - 1, total.shape[1]), jnp.float32)
        for part, ref in enumerate((keep_ref, send_ref)):
            def chunk(c, carry, part=part, ref=ref):
                first = where_[part * chunks + c]
                rows = []
                for p in range(pairs):
                    rows.append(
                        jnp.concatenate(
                            [gacc[pl.ds(first + 2 * p, 1), :], gacc[pl.ds(first + 2 * p + 1, 1), :]], axis=1
                        )
                    )
                ref[c] = jnp.concatenate(rows + [diag_ref[part, c], total, rest], axis=0)
                return carry

            lax.fori_loop(0, chunks, chunk, 0)


def solve_body(damp, a_ref, b_ref, out_ref, mis_ref):
    x = a_ref[...] + b_ref[...]
    width = x.shape[1]
    blk = width // 2
    half = blk // 2
    pairs = (x.shape[0] - EXTRA) // half
    ext = x[pairs * half :]
    mis_ref[...] = jnp.broadcast_to(jnp.sum(ext[2 * pairs : 2 * pairs + 1], axis=1, keepdims=True), mis_ref.shape)
    row = lax.broadcasted_iota(jnp.int32, (half, width), 0)
    lane = lax.broadcasted_iota(jnp.int32, (half, width), 1)
    frow = lax.broadcasted_iota(jnp.int32, (blk, width), 0)
    flane = lax.broadcasted_iota(jnp.int32, (blk, width), 1)
    eye = frow == flane
    scale = damp[0]
    mats = []
    diags = []
    for p in range(pairs):
        for odd in range(2):
            t = x[p * half : (p + 1) * half]
            grad = ext[p : p + 1]
            diag = ext[pairs + p : pairs + p + 1]
            if odd:
                t = pltpu.roll(t, blk, 1)
                grad = pltpu.roll(grad, blk, 1)
                diag = pltpu.roll(diag, blk, 1)
            tt = jnp.concatenate([t, jnp.zeros((width - half, width), jnp.float32)], axis=0).T
            mt = tt[:half]
            top = jnp.where((lane < half) & (row > lane), mt, t)
            low = jnp.where(row > lane - half, pltpu.roll(t, half, 1), pltpu.roll(mt, half, 1))
            bot = jnp.where(lane < half, tt[half:blk], low)
            full = jnp.concatenate([top, bot], axis=0)
            full = jnp.where(eye, (diag + scale * diag) + 1.0, full)
            col = jnp.sum(jnp.where(eye, jnp.broadcast_to(grad, (blk, width)), 0.0), axis=1, keepdims=True)
            full = jnp.where(flane == blk, col, full)
            mats.append([full[8 * i : 8 * i + 8] for i in range(blk // 8)])
            diags.append(diag)
    sub = lax.broadcasted_iota(jnp.int32, (8, width), 0)
    for k in range(blk):
        own, at = divmod(k, 8)
        for m in mats:
            prow = m[own][at : at + 1, :]
            prow = prow / prow[:, k : k + 1]
            for i in range(blk // 8):
                new = m[i] - m[i][:, k : k + 1] * prow
                m[i] = jnp.where(sub == at, prow, new) if i == own else new
    lines = []
    for m, diag in zip(mats, diags):
        line = jnp.zeros((8, width), jnp.float32)
        for i in range(blk // 8):
            line = line + jnp.where(eye[8 * i : 8 * i + 8], m[i][:, blk : blk + 1], 0.0)
        lines.append(jnp.sum(line, axis=0, keepdims=True) * jnp.sqrt(diag))
    out_ref[...] = jnp.concatenate(lines, axis=0)


def fast(observed, jacobian, tile_block, params, damping):
    ngx, ngy = lax.axis_size("gx"), lax.axis_size("gy")
    tiles, blk, vox = jacobian.shape
    per = NB // (ngx * ngy)
    half = blk // 2
    pairs = per // 2
    rows = pairs * half + EXTRA
    moved = flipped(observed, ("gx", "gy"), ngx * ngy)[::-1, ::-1]
    bits = ngx.bit_length() - 1
    rel = jnp.arange(ngx, dtype=jnp.int32)
    owner = jnp.zeros_like(rel)
    for s in range(bits):
        owner = owner | (((rel >> (bits - 1 - s)) & 1) << s)
    owner = owner ^ lax.axis_index("gx")
    me_y = lax.axis_index("gy")
    where_ = per * jnp.concatenate([me_y * ngx + owner, (1 - me_y) * ngx + owner])

    steps = tiles // STEP_TILES
    payload = jax.ShapeDtypeStruct((ngx, rows, vox), jnp.float32)
    whole = lambda *shape: pl.BlockSpec(shape, lambda s, *_: (0,) * len(shape))
    jspec = pl.BlockSpec((STEP_TILES, blk, vox), lambda s, *_: (s, 0, 0))
    tspec = pl.BlockSpec((STEP_TILES, vox), lambda s, *_: (s, 0))
    calc, keep, send, diag = pl.pallas_call(
        gram_body,
        out_shape=(
            jax.ShapeDtypeStruct((tiles, vox), jnp.float32),
            payload,
            payload,
            jax.ShapeDtypeStruct((2, ngx, pairs, vox), jnp.float32),
        ),
        grid_spec=pltpu.PrefetchScalarGridSpec(
            num_scalar_prefetch=2,
            grid=(steps,),
            in_specs=[jspec, whole(NB, blk)],
            out_specs=(tspec, whole(ngx, rows, vox), whole(ngx, rows, vox), whole(2, ngx, pairs, vox)),
            scratch_shapes=[pltpu.VMEM((NB, blk, blk), jnp.float32)],
        ),
        name="gram",
    )(tile_block, where_, jacobian, params)
    espec = pl.BlockSpec((ngx, EXTRA, vox), lambda s, *_: (0, (rows - EXTRA) // EXTRA, 0))
    hbm = pl.BlockSpec(memory_space=pl.ANY)
    keep, send = pl.pallas_call(
        grad_body,
        out_shape=(payload, payload),
        grid_spec=pltpu.PrefetchScalarGridSpec(
            num_scalar_prefetch=2,
            grid=(steps,),
            in_specs=[jspec, tspec, tspec, tspec, whole(2, ngx, pairs, vox), hbm, hbm],
            out_specs=(espec, espec),
            scratch_shapes=[pltpu.VMEM((NB, blk), jnp.float32), pltpu.VMEM((GROUP, vox), jnp.float32)],
        ),
        input_output_aliases={7: 0, 8: 1},
        name="grad",
    )(tile_block, where_, jacobian, calc, observed, moved, diag, keep, send)

    mine, got = keep, xored(send, "gy", 1)
    for s in range(bits):
        both = mine + got
        n = both.shape[0] // 2
        mine, got = both[:n], xored(both[n:], "gx", 1 << s)
    smem = pl.BlockSpec(memory_space=pltpu.SMEM)
    vmem = pl.BlockSpec(memory_space=pltpu.VMEM)
    step, misfit = pl.pallas_call(
        solve_body,
        out_shape=(jax.ShapeDtypeStruct((per, vox), jnp.float32), jax.ShapeDtypeStruct((8, vox), jnp.float32)),
        in_specs=[smem, vmem, vmem],
        out_specs=(vmem, vmem),
        name="solve",
    )(damping, mine[0], got[0])
    every = lax.all_to_all(jnp.broadcast_to(step[None], (ngx, per, vox)), "gx", 0, 0)
    return every.reshape(ngx * per, vox)[:, :blk], misfit[0, 0] / (tiles * ngx * ngy * vox)


def solve_blocks(system, rhs):
    size = system.shape[1]
    augmented = jnp.concatenate([system, rhs[:, :, None]], axis=2)
    augmented = jnp.transpose(augmented, (1, 2, 0))
    row_ids = jnp.arange(size, dtype=jnp.int32)

    def eliminate(step, current):
        column = step.astype(jnp.int32)
        pivot_row = lax.dynamic_index_in_dim(current, column, 0, keepdims=False)
        pivot = lax.dynamic_index_in_dim(pivot_row, column, 0, keepdims=False)
        pivot_row = pivot_row / pivot[None, :]
        factors = lax.dynamic_index_in_dim(current, column, 1, keepdims=False)
        updated = current - factors[:, None, :] * pivot_row[None, :, :]
        is_pivot = (row_ids == column)[:, None, None]
        return jnp.where(is_pivot, pivot_row[None, :, :], updated)

    final = lax.fori_loop(0, size, eliminate, augmented)
    return jnp.transpose(final[:, size, :], (1, 0))


def general(observed, jacobian, tile_block, params, damping):
    ngx, ngy = lax.axis_size("gx"), lax.axis_size("gy")
    moved = flipped(observed, ("gx", "gy"), ngx * ngy)[::-1, ::-1]
    block_ids = jnp.arange(NB, dtype=jnp.int32)
    onehot = (tile_block[:, None] == block_ids[None, :]).astype(jnp.float32)
    tile_params = jnp.dot(onehot, params, precision=lax.Precision.HIGHEST).astype(jnp.bfloat16)
    calc = jnp.einsum("tpv,tp->tv", jacobian, tile_params, preferred_element_type=jnp.float32)
    resid = 0.5 * (observed + moved) - calc
    local_misfit = jnp.sum(resid * resid)
    resid_b = resid.astype(jnp.bfloat16)
    tile_grad = jnp.einsum("tpv,tv->tp", jacobian, resid_b, preferred_element_type=jnp.float32)
    tile_gram = jnp.einsum("tpv,tqv->tpq", jacobian, jacobian, preferred_element_type=jnp.float32)
    gram = jnp.einsum("tb,tpq->bpq", onehot, tile_gram, precision=lax.Precision.HIGHEST)
    grad = jnp.dot(onehot.T, tile_grad, precision=lax.Precision.HIGHEST)
    owned = NB // ngy
    gram, grad, total = lax.psum((gram, grad, local_misfit), ("gx", "gy"))
    first = lax.axis_index("gy") * owned
    gram = lax.dynamic_slice_in_dim(gram, first, owned, 0)
    grad = lax.dynamic_slice_in_dim(grad, first, owned, 0)
    diagonal = jnp.diagonal(gram, axis1=1, axis2=2)
    eye = jnp.eye(gram.shape[1], dtype=jnp.float32)
    system = gram + damping[0] * diagonal[:, :, None] * eye[None] + eye[None]
    delta = solve_blocks(system, grad)
    return delta * jnp.sqrt(diagonal), total / (observed.size * ngx * ngy)


def solution(mesh):
    ngx, ngy = mesh.shape["gx"], mesh.shape["gy"]
    quick = ngy == 2 and ngx & (ngx - 1) == 0 and NB % (2 * ngx * ngy) == 0
    return jax.shard_map(
        fast if quick else general,
        mesh=mesh,
        in_specs=(P(("gx", "gy"), None), P(("gx", "gy"), None, None), P(("gx", "gy")), P(), P()),
        out_specs=(P("gy", None), P()),
        check_vma=False,
    )
```

```python
import jax
import jax.numpy as jnp
from jax import lax
from jax.experimental import pallas as pl
from jax.experimental.pallas import tpu as pltpu
from jax.sharding import PartitionSpec as P

NB = 128
STEP_TILES = 32
GROUP = 8
EXTRA = 8


def flipped(value, axes, size):
    return lax.ppermute(value, axes, [(i, size - 1 - i) for i in range(size)])


def xored(value, axis, bit):
    return lax.ppermute(value, axis, [(i, i ^ bit) for i in range(lax.axis_size(axis))])


def nt_dot(a, b):
    return lax.dot_general(a, b, (((1,), (1,)), ((), ())), preferred_element_type=jnp.float32)


def gathered(value, index, axis):
    return jnp.take_along_axis(value, index, axis=axis, mode="promise_in_bounds")


def owner_of(c, chunks):
    bits = chunks.bit_length() - 1
    swapped = sum(((c >> (bits - 1 - s)) & 1) << s for s in range(bits))
    return swapped ^ lax.axis_index("gx")


def first_block(part, c, chunks, per):
    side = lax.axis_index("gy")
    return per * ((side if part == 0 else 1 - side) * chunks + owner_of(c, chunks))


def gram_body(tb, j_ref, par_ref, calc_ref, keep_ref, send_ref, diag_ref, acc, par):
    step = pl.program_id(0)
    blk, vox = j_ref.shape[1:]
    half = blk // 2

    @pl.when(step == 0)
    def _():
        acc[...] = jnp.zeros_like(acc)
        par[...] = par_ref[...].astype(jnp.bfloat16).astype(jnp.float32)

    zero = jnp.zeros((blk, vox), jnp.bfloat16)
    low = lax.broadcasted_iota(jnp.int32, (blk, 2 * blk), 1) < blk

    def group(g, carry):
        base = g * GROUP
        rows = []
        for u in range(0, GROUP, 2):
            left, right = j_ref[base + u], j_ref[base + u + 1]
            lhs = jnp.concatenate([left, right], axis=1)
            rhs = jnp.concatenate(
                [jnp.concatenate([left, zero], axis=1), jnp.concatenate([zero, right], axis=1)], axis=0
            )
            gram = nt_dot(lhs, rhs)
            for v, jac in enumerate((left, right)):
                b = tb[step * STEP_TILES + base + u + v]
                pltpu.store(acc.at[b], acc[b] + gram, mask=low if v == 0 else jnp.logical_not(low))
                spread = gathered(par[...], jnp.full((blk, vox), b, jnp.int32), 1)
                rows.append(jnp.sum(jac.astype(jnp.float32) * spread, axis=0, keepdims=True))
        calc_ref[pl.ds(pl.multiple_of(base, GROUP), GROUP), :] = jnp.concatenate(rows, axis=0)
        return carry

    lax.fori_loop(0, STEP_TILES // GROUP, group, 0)

    @pl.when(step == pl.num_programs(0) - 1)
    def _():
        chunks = keep_ref.shape[0]
        pairs = (keep_ref.shape[1] - EXTRA) // half
        row = lax.broadcasted_iota(jnp.int32, (half, 2 * blk), 0)
        lane = lax.broadcasted_iota(jnp.int32, (half, 2 * blk), 1) % blk
        use_bot = (lane < half) & (row > lane)
        frow = lax.broadcasted_iota(jnp.int32, (blk, 2 * blk), 0)
        flane = lax.broadcasted_iota(jnp.int32, (blk, 2 * blk), 1) % blk
        on_diag = frow == flane
        for part, ref in enumerate((keep_ref, send_ref)):
            def chunk(c, carry, part=part, ref=ref):
                first = first_block(part, c, chunks, 2 * pairs)
                for p in range(pairs):
                    one, two = acc[first + 2 * p], acc[first + 2 * p + 1]
                    full = jnp.where(low, one, two) + pltpu.roll(jnp.where(low, two, one), blk, 1)
                    bot = pltpu.roll(full[half:], 2 * blk - half, 1)
                    ref[c, p * half : (p + 1) * half, :] = jnp.where(use_bot, bot, full[:half])
                    diag_ref[part, c, p : p + 1, :] = jnp.sum(
                        jnp.where(on_diag, full, 0.0), axis=0, keepdims=True
                    )
                return carry

            lax.fori_loop(0, chunks, chunk, 0)


def grad_body(tb, j_ref, calc_ref, obs_ref, mir_ref, diag_ref, keep_in, send_in, keep_ref, send_ref, gacc, mis, mix):
    step = pl.program_id(0)
    blk, vox = j_ref.shape[1:]

    @pl.when(step == 0)
    def _():
        gacc[...] = jnp.zeros_like(gacc)
        mis[...] = jnp.zeros_like(mis)

    back = vox - 1 - lax.broadcasted_iota(jnp.int32, (GROUP, vox), 1)
    up = GROUP - 1 - lax.broadcasted_iota(jnp.int32, (GROUP, vox), 0)
    lane = lax.broadcasted_iota(jnp.int32, (blk, vox), 1)

    def group(g, carry):
        base = pl.multiple_of(g * GROUP, GROUP)
        rows = pl.ds(base, GROUP)
        mirror = mir_ref[pl.ds(pl.multiple_of(STEP_TILES - GROUP - base, GROUP), GROUP), :]
        mirror = gathered(gathered(mirror, back, 1), up, 0)
        resid = 0.5 * (obs_ref[rows, :] + mirror) - calc_ref[rows, :]
        mis[...] += resid * resid
        resid_b = resid.astype(jnp.bfloat16).astype(jnp.float32)
        total = gacc[...]
        for u in range(GROUP):
            b = tb[step * STEP_TILES + base + u]
            grad = jnp.sum(j_ref[base + u].astype(jnp.float32) * resid_b[u : u + 1], axis=1, keepdims=True)
            total = total + jnp.where(lane == b, grad, 0.0)
        gacc[...] = total
        return carry

    lax.fori_loop(0, STEP_TILES // GROUP, group, 0)

    @pl.when(step == pl.num_programs(0) - 1)
    def _():
        chunks = keep_ref.shape[0]
        pairs = diag_ref.shape[2]
        total = jnp.sum(mis[...], axis=0, keepdims=True)
        rest = jnp.zeros((EXTRA - 2 * pairs - 1, vox), jnp.float32)
        wide = jnp.concatenate([gacc[...], jnp.zeros((vox - blk, vox), jnp.float32)], axis=0).T
        by_block = wide + pltpu.roll(wide, blk, 1)
        odd = (lax.broadcasted_iota(jnp.int32, by_block.shape, 0) % 2) == 1
        high = lax.broadcasted_iota(jnp.int32, by_block.shape, 1) >= blk
        spread = jnp.where(odd == high, by_block, 0.0)
        mix[...] = spread
        for part, ref in enumerate((keep_ref, send_ref)):
            def chunk(c, carry, part=part, ref=ref):
                first = first_block(part, c, chunks, 2 * pairs)
                rows = [
                    mix[pl.ds(first + 2 * p, 1), :] + mix[pl.ds(first + 2 * p + 1, 1), :] for p in range(pairs)
                ]
                ref[c] = jnp.concatenate(rows + [diag_ref[part, c], total, rest], axis=0)
                return carry

            lax.fori_loop(0, chunks, chunk, 0)


def solve_body(damp, a_ref, b_ref, out_ref, mis_ref):
    x = a_ref[...] + b_ref[...]
    width = x.shape[1]
    blk = width // 2
    half = blk // 2
    tall = blk // 8
    pairs = (x.shape[0] - EXTRA) // half
    ext = x[pairs * half :]
    mis_ref[...] = jnp.broadcast_to(jnp.sum(ext[2 * pairs : 2 * pairs + 1], axis=1, keepdims=True), mis_ref.shape)
    row = lax.broadcasted_iota(jnp.int32, (half, width), 0)
    lane = lax.broadcasted_iota(jnp.int32, (half, width), 1)
    inner = lane % blk
    frow = lax.broadcasted_iota(jnp.int32, (blk, width), 0)
    flane = lax.broadcasted_iota(jnp.int32, (blk, width), 1)
    eye = frow == flane % blk
    scale = damp[0]
    mats = []
    rights = []
    diags = []
    for p in range(pairs):
        t = x[p * half : (p + 1) * half]
        grad = ext[p : p + 1]
        diag = ext[pairs + p : pairs + p + 1]
        tt = jnp.concatenate([t, jnp.zeros((width - half, width), jnp.float32)], axis=0).T
        mt = jnp.where(lane < blk, tt[:half], pltpu.roll(tt[blk : blk + half], blk, 1))
        bt = jnp.where(lane < blk, tt[half:blk], pltpu.roll(tt[blk + half :], blk, 1))
        top = jnp.where((inner < half) & (row > inner), mt, t)
        low = jnp.where(row > inner - half, pltpu.roll(t, half, 1), pltpu.roll(mt, half, 1))
        full = jnp.concatenate([top, jnp.where(inner < half, bt, low)], axis=0)
        full = jnp.where(eye, (diag + scale * diag) + 1.0, full)
        cols = jnp.where(eye, jnp.broadcast_to(grad, (blk, width)), 0.0)
        right = jnp.where(
            flane < blk,
            jnp.sum(jnp.where(flane < blk, cols, 0.0), axis=1, keepdims=True),
            jnp.sum(jnp.where(flane < blk, 0.0, cols), axis=1, keepdims=True),
        )
        mats.append([full[8 * i : 8 * i + 8] for i in range(tall)])
        rights.append([right[8 * i : 8 * i + 8] for i in range(tall)])
        diags.append(diag)
    sub = lax.broadcasted_iota(jnp.int32, (8, width), 0)
    lanes = lax.broadcasted_iota(jnp.int32, (8, width), 1)
    side = lanes - lanes % blk
    for k in range(blk):
        own, at = divmod(k, 8)
        for m, right in zip(mats, rights):
            factors = [gathered(m[i], side + k, 1) for i in range(tall)]
            pivot = factors[own][at : at + 1, :]
            prow = m[own][at : at + 1, :] / pivot
            for i in range(tall):
                new = m[i] - factors[i] * prow
                m[i] = jnp.where(sub == at, prow, new) if i == own else new
            if k == 0:
                rrow = right[0][:1, :] / pivot
                for i in range(tall):
                    new = right[i] - factors[i] * rrow
                    new = jnp.where(sub == 0, rrow, new) if i == 0 else new
                    m[i] = jnp.where(lanes == side, new, m[i])
    lines = []
    for m, diag in zip(mats, diags):
        line = jnp.zeros((8, width), jnp.float32)
        for i in range(tall):
            line = line + jnp.where(eye[8 * i : 8 * i + 8], gathered(m[i], side, 1), 0.0)
        line = jnp.sum(line, axis=0, keepdims=True) * jnp.sqrt(diag)
        lines += [line, pltpu.roll(line, blk, 1)]
    out = jnp.concatenate(lines, axis=0)
    for c in range(out_ref.shape[0]):
        out_ref[c] = out


def fast(observed, jacobian, tile_block, params, damping):
    ngx, ngy = lax.axis_size("gx"), lax.axis_size("gy")
    tiles, blk, vox = jacobian.shape
    per = NB // (ngx * ngy)
    half = blk // 2
    pairs = per // 2
    rows = pairs * half + EXTRA
    moved = flipped(observed, ("gx", "gy"), ngx * ngy)
    bits = ngx.bit_length() - 1
    steps = tiles // STEP_TILES
    payload = jax.ShapeDtypeStruct((ngx, rows, vox), jnp.float32)
    whole = lambda *shape: pl.BlockSpec(shape, lambda s, *_: (0,) * len(shape))
    jspec = pl.BlockSpec((STEP_TILES, blk, vox), lambda s, *_: (s, 0, 0))
    mspec = pl.BlockSpec((STEP_TILES, vox), lambda s, *_: (steps - 1 - s, 0))
    tspec = pl.BlockSpec((STEP_TILES, vox), lambda s, *_: (s, 0))
    calc, keep, send, diag = pl.pallas_call(
        gram_body,
        out_shape=(
            jax.ShapeDtypeStruct((tiles, vox), jnp.float32),
            payload,
            payload,
            jax.ShapeDtypeStruct((2, ngx, pairs, vox), jnp.float32),
        ),
        grid_spec=pltpu.PrefetchScalarGridSpec(
            num_scalar_prefetch=1,
            grid=(steps,),
            in_specs=[jspec, whole(blk, NB)],
            out_specs=(tspec, whole(ngx, rows, vox), whole(ngx, rows, vox), whole(2, ngx, pairs, vox)),
            scratch_shapes=[pltpu.VMEM((NB, blk, 2 * blk), jnp.float32), pltpu.VMEM((blk, NB), jnp.float32)],
        ),
        name="gram",
    )(tile_block, jacobian, params.T)
    espec = pl.BlockSpec((ngx, EXTRA, vox), lambda s, *_: (0, (rows - EXTRA) // EXTRA, 0))
    hbm = pl.BlockSpec(memory_space=pl.ANY)
    keep, send = pl.pallas_call(
        grad_body,
        out_shape=(payload, payload),
        grid_spec=pltpu.PrefetchScalarGridSpec(
            num_scalar_prefetch=1,
            grid=(steps,),
            in_specs=[jspec, tspec, tspec, mspec, whole(2, ngx, pairs, vox), hbm, hbm],
            out_specs=(espec, espec),
            scratch_shapes=[
                pltpu.VMEM((blk, NB), jnp.float32),
                pltpu.VMEM((GROUP, vox), jnp.float32),
                pltpu.VMEM((NB, vox), jnp.float32),
            ],
        ),
        input_output_aliases={6: 0, 7: 1},
        name="grad",
    )(tile_block, jacobian, calc, observed, moved, diag, keep, send)

    mine, got = keep, xored(send, "gy", 1)
    for s in range(bits):
        both = mine + got
        n = both.shape[0] // 2
        mine, got = both[:n], xored(both[n:], "gx", 1 << s)
    smem = pl.BlockSpec(memory_space=pltpu.SMEM)
    vmem = pl.BlockSpec(memory_space=pltpu.VMEM)
    step, misfit = pl.pallas_call(
        solve_body,
        out_shape=(jax.ShapeDtypeStruct((ngx, per, vox), jnp.float32), jax.ShapeDtypeStruct((8, vox), jnp.float32)),
        in_specs=[smem, vmem, vmem],
        out_specs=(vmem, vmem),
        name="solve",
    )(damping, mine[0], got[0])
    every = lax.all_to_all(step, "gx", 0, 0)
    return every.reshape(ngx * per, vox)[:, :blk], misfit[0, 0] / (tiles * ngx * ngy * vox)


def solve_blocks(system, rhs):
    size = system.shape[1]
    augmented = jnp.concatenate([system, rhs[:, :, None]], axis=2)
    augmented = jnp.transpose(augmented, (1, 2, 0))
    row_ids = jnp.arange(size, dtype=jnp.int32)

    def eliminate(step, current):
        column = step.astype(jnp.int32)
        pivot_row = lax.dynamic_index_in_dim(current, column, 0, keepdims=False)
        pivot = lax.dynamic_index_in_dim(pivot_row, column, 0, keepdims=False)
        pivot_row = pivot_row / pivot[None, :]
        factors = lax.dynamic_index_in_dim(current, column, 1, keepdims=False)
        updated = current - factors[:, None, :] * pivot_row[None, :, :]
        is_pivot = (row_ids == column)[:, None, None]
        return jnp.where(is_pivot, pivot_row[None, :, :], updated)

    final = lax.fori_loop(0, size, eliminate, augmented)
    return jnp.transpose(final[:, size, :], (1, 0))


def general(observed, jacobian, tile_block, params, damping):
    ngx, ngy = lax.axis_size("gx"), lax.axis_size("gy")
    moved = flipped(observed, ("gx", "gy"), ngx * ngy)[::-1, ::-1]
    block_ids = jnp.arange(NB, dtype=jnp.int32)
    onehot = (tile_block[:, None] == block_ids[None, :]).astype(jnp.float32)
    tile_params = jnp.dot(onehot, params, precision=lax.Precision.HIGHEST).astype(jnp.bfloat16)
    calc = jnp.einsum("tpv,tp->tv", jacobian, tile_params, preferred_element_type=jnp.float32)
    resid = 0.5 * (observed + moved) - calc
    local_misfit = jnp.sum(resid * resid)
    resid_b = resid.astype(jnp.bfloat16)
    tile_grad = jnp.einsum("tpv,tv->tp", jacobian, resid_b, preferred_element_type=jnp.float32)
    tile_gram = jnp.einsum("tpv,tqv->tpq", jacobian, jacobian, preferred_element_type=jnp.float32)
    gram = jnp.einsum("tb,tpq->bpq", onehot, tile_gram, precision=lax.Precision.HIGHEST)
    grad = jnp.dot(onehot.T, tile_grad, precision=lax.Precision.HIGHEST)
    owned = NB // ngy
    gram, grad, total = lax.psum((gram, grad, local_misfit), ("gx", "gy"))
    first = lax.axis_index("gy") * owned
    gram = lax.dynamic_slice_in_dim(gram, first, owned, 0)
    grad = lax.dynamic_slice_in_dim(grad, first, owned, 0)
    diagonal = jnp.diagonal(gram, axis1=1, axis2=2)
    eye = jnp.eye(gram.shape[1], dtype=jnp.float32)
    system = gram + damping[0] * diagonal[:, :, None] * eye[None] + eye[None]
    delta = solve_blocks(system, grad)
    return delta * jnp.sqrt(diagonal), total / (observed.size * ngx * ngy)


def solution(mesh):
    ngx, ngy = mesh.shape["gx"], mesh.shape["gy"]
    quick = ngy == 2 and ngx & (ngx - 1) == 0 and NB % (2 * ngx * ngy) == 0
    return jax.shard_map(
        fast if quick else general,
        mesh=mesh,
        in_specs=(P(("gx", "gy"), None), P(("gx", "gy"), None, None), P(("gx", "gy")), P(), P()),
        out_specs=(P("gy", None), P()),
        check_vma=False,
    )
```

```python
import jax
import jax.numpy as jnp
from jax import lax
from jax.experimental import pallas as pl
from jax.experimental.pallas import tpu as pltpu
from jax.sharding import PartitionSpec as P

NB = 128
STEP_TILES = 64
GROUP = 8
GRAM_UNROLL = 4
GRAD_UNROLL = 4
PACK_UNROLL = 4
PANEL = 8
EXTRA = 8
PLANE = 4


def flipped(value, axes, size):
    return lax.ppermute(value, axes, [(i, size - 1 - i) for i in range(size)])


def xored(value, axis, bit):
    return lax.ppermute(value, axis, [(i, i ^ bit) for i in range(lax.axis_size(axis))])


def plane(value):
    parts = value.reshape(PLANE, value.shape[0] // PLANE, *value.shape[1:])
    total = parts[0]
    for k in range(1, PLANE):
        total = total + xored(parts[k], "gx", k)
    return total


def nt_dot(a, b):
    return lax.dot_general(a, b, (((1,), (1,)), ((), ())), preferred_element_type=jnp.float32)


def gathered(value, index, axis):
    return jnp.take_along_axis(value, index, axis=axis, mode="promise_in_bounds")


def owner_of(c, chunks):
    line = chunks // PLANE
    bits = line.bit_length() - 1
    far = c % line
    swapped = sum(((far >> (bits - 1 - s)) & 1) << s for s in range(bits))
    return (c // line + PLANE * swapped) ^ lax.axis_index("gx")


def first_block(part, c, chunks, per):
    side = lax.axis_index("gy")
    return per * ((side if part == 0 else 1 - side) * chunks + owner_of(c, chunks))


def gram_body(tb, j_ref, par_ref, calc_ref, keep_ref, send_ref, diag_ref, acc, par):
    step = pl.program_id(0)
    blk, vox = j_ref.shape[1:]
    half = blk // 2

    @pl.when(step == 0)
    def _():
        acc[...] = jnp.zeros_like(acc)
        par[...] = par_ref[...].astype(jnp.bfloat16).astype(jnp.float32)

    zero = jnp.zeros((blk, vox), jnp.bfloat16)
    low = lax.broadcasted_iota(jnp.int32, (blk, 2 * blk), 1) < blk

    def group(g, carry):
        base = g * GROUP
        rows = []
        for u in range(0, GROUP, 2):
            left, right = j_ref[base + u], j_ref[base + u + 1]
            lhs = jnp.concatenate([left, right], axis=1)
            rhs = jnp.concatenate(
                [jnp.concatenate([left, zero], axis=1), jnp.concatenate([zero, right], axis=1)], axis=0
            )
            gram = nt_dot(lhs, rhs)
            for v, jac in enumerate((left, right)):
                b = tb[step * STEP_TILES + base + u + v]
                pltpu.store(acc.at[b], acc[b] + gram, mask=low if v == 0 else jnp.logical_not(low))
                spread = gathered(par[...], jnp.full((blk, vox), b, jnp.int32), 1)
                rows.append(jnp.sum(jac.astype(jnp.float32) * spread, axis=0, keepdims=True))
        calc_ref[pl.ds(pl.multiple_of(base, GROUP), GROUP), :] = jnp.concatenate(rows, axis=0)
        return carry

    lax.fori_loop(0, STEP_TILES // GROUP, group, 0, unroll=GRAM_UNROLL)

    @pl.when(step == pl.num_programs(0) - 1)
    def _():
        chunks = keep_ref.shape[0]
        pairs = keep_ref.shape[1] // half
        row = lax.broadcasted_iota(jnp.int32, (half, 2 * blk), 0)
        lane = lax.broadcasted_iota(jnp.int32, (half, 2 * blk), 1) % blk
        use_bot = (lane < half) & (row > lane)
        frow = lax.broadcasted_iota(jnp.int32, (blk, 2 * blk), 0)
        flane = lax.broadcasted_iota(jnp.int32, (blk, 2 * blk), 1) % blk
        on_diag = frow == flane
        for part, ref in enumerate((keep_ref, send_ref)):
            def chunk(c, carry, part=part, ref=ref):
                first = first_block(part, c, chunks, 2 * pairs)
                for p in range(pairs):
                    one, two = acc[first + 2 * p], acc[first + 2 * p + 1]
                    full = jnp.where(low, one, two) + pltpu.roll(jnp.where(low, two, one), blk, 1)
                    bot = pltpu.roll(full[half:], 2 * blk - half, 1)
                    ref[c, p * half : (p + 1) * half, :] = jnp.where(use_bot, bot, full[:half])
                    diag_ref[part, c, p : p + 1, :] = jnp.sum(
                        jnp.where(on_diag, full, 0.0), axis=0, keepdims=True
                    )
                return carry

            lax.fori_loop(0, chunks, chunk, 0, unroll=PACK_UNROLL)


def grad_body(tb, j_ref, calc_ref, obs_ref, mir_ref, diag_ref, keep_ref, send_ref, gacc, mis, mix):
    step = pl.program_id(0)
    blk, vox = j_ref.shape[1:]

    @pl.when(step == 0)
    def _():
        gacc[...] = jnp.zeros_like(gacc)
        mis[...] = jnp.zeros_like(mis)

    back = vox - 1 - lax.broadcasted_iota(jnp.int32, (GROUP, vox), 1)
    up = GROUP - 1 - lax.broadcasted_iota(jnp.int32, (GROUP, vox), 0)
    lane = lax.broadcasted_iota(jnp.int32, (blk, vox), 1)

    def group(g, carry):
        base = pl.multiple_of(g * GROUP, GROUP)
        rows = pl.ds(base, GROUP)
        mirror = mir_ref[pl.ds(pl.multiple_of(STEP_TILES - GROUP - base, GROUP), GROUP), :]
        mirror = gathered(gathered(mirror, back, 1), up, 0)
        resid = 0.5 * (obs_ref[rows, :] + mirror) - calc_ref[rows, :]
        mis[...] += resid * resid
        resid_b = resid.astype(jnp.bfloat16).astype(jnp.float32)
        total = gacc[...]
        for u in range(GROUP):
            b = tb[step * STEP_TILES + base + u]
            grad = jnp.sum(j_ref[base + u].astype(jnp.float32) * resid_b[u : u + 1], axis=1, keepdims=True)
            total = total + jnp.where(lane == b, grad, 0.0)
        gacc[...] = total
        return carry

    lax.fori_loop(0, STEP_TILES // GROUP, group, 0, unroll=GRAD_UNROLL)

    @pl.when(step == pl.num_programs(0) - 1)
    def _():
        chunks = keep_ref.shape[0]
        pairs = diag_ref.shape[2]
        total = jnp.sum(mis[...], axis=0, keepdims=True)
        rest = jnp.zeros((EXTRA - 2 * pairs - 1, vox), jnp.float32)
        wide = jnp.concatenate([gacc[...], jnp.zeros((vox - blk, vox), jnp.float32)], axis=0).T
        by_block = wide + pltpu.roll(wide, blk, 1)
        odd = (lax.broadcasted_iota(jnp.int32, by_block.shape, 0) % 2) == 1
        high = lax.broadcasted_iota(jnp.int32, by_block.shape, 1) >= blk
        spread = jnp.where(odd == high, by_block, 0.0)
        mix[...] = spread
        for part, ref in enumerate((keep_ref, send_ref)):
            def chunk(c, carry, part=part, ref=ref):
                first = first_block(part, c, chunks, 2 * pairs)
                rows = [
                    mix[pl.ds(first + 2 * p, 1), :] + mix[pl.ds(first + 2 * p + 1, 1), :] for p in range(pairs)
                ]
                ref[c] = jnp.concatenate(rows + [diag_ref[part, c], total, rest], axis=0)
                return carry

            lax.fori_loop(0, chunks, chunk, 0, unroll=PACK_UNROLL)


def solve_body(damp, a_ref, b_ref, out_ref, mis_ref):
    x = a_ref[...] + b_ref[...]
    width = x.shape[1]
    blk = width // 2
    half = blk // 2
    tall = blk // 8
    pairs = (x.shape[0] - EXTRA) // half
    ext = x[pairs * half :]
    mis_ref[...] = jnp.broadcast_to(jnp.sum(ext[2 * pairs : 2 * pairs + 1], axis=1, keepdims=True), mis_ref.shape)
    row = lax.broadcasted_iota(jnp.int32, (half, width), 0)
    lane = lax.broadcasted_iota(jnp.int32, (half, width), 1)
    inner = lane % blk
    frow = lax.broadcasted_iota(jnp.int32, (blk, width), 0)
    flane = lax.broadcasted_iota(jnp.int32, (blk, width), 1)
    eye = frow == flane % blk
    scale = damp[0]
    mats = []
    rights = []
    diags = []
    for p in range(pairs):
        t = x[p * half : (p + 1) * half]
        grad = ext[p : p + 1]
        diag = ext[pairs + p : pairs + p + 1]
        tt = jnp.concatenate([t, jnp.zeros((width - half, width), jnp.float32)], axis=0).T
        mt = jnp.where(lane < blk, tt[:half], pltpu.roll(tt[blk : blk + half], blk, 1))
        bt = jnp.where(lane < blk, tt[half:blk], pltpu.roll(tt[blk + half :], blk, 1))
        top = jnp.where((inner < half) & (row > inner), mt, t)
        low = jnp.where(row > inner - half, pltpu.roll(t, half, 1), pltpu.roll(mt, half, 1))
        full = jnp.concatenate([top, jnp.where(inner < half, bt, low)], axis=0)
        full = jnp.where(eye, (diag + scale * diag) + 1.0, full)
        cols = jnp.where(eye, jnp.broadcast_to(grad, (blk, width)), 0.0)
        right = jnp.where(
            flane < blk,
            jnp.sum(jnp.where(flane < blk, cols, 0.0), axis=1, keepdims=True),
            jnp.sum(jnp.where(flane < blk, 0.0, cols), axis=1, keepdims=True),
        )
        mats.append([full[8 * i : 8 * i + 8] for i in range(tall)])
        rights.append([right[8 * i : 8 * i + 8] for i in range(tall)])
        diags.append(diag)
    sub = lax.broadcasted_iota(jnp.int32, (8, width), 0)
    lanes = lax.broadcasted_iota(jnp.int32, (8, width), 1)
    side = lanes - lanes % blk
    for k in range(0, blk, PANEL):
        own = k // 8
        for m, right in zip(mats, rights):
            cols = [[gathered(m[i], side + (k + j), 1) for i in range(tall)] for j in range(PANEL)]
            if k == 0:
                cols.append(right)
            for j in range(PANEL):
                at = (k + j) % 8
                pivot = jnp.broadcast_to(cols[j][own][at : at + 1], (8, width))

                def eliminate(part):
                    prow = jnp.broadcast_to(part[own][at : at + 1], (8, width)) / pivot
                    new = [part[i] - cols[j][i] * prow for i in range(tall)]
                    new[own] = jnp.where(sub == at, prow, new[own])
                    return new

                cols[j + 1 :] = [eliminate(col) for col in cols[j + 1 :]]
                m[:] = eliminate(m)
            if k == 0:
                m[:] = [jnp.where(lanes == side, cols[PANEL][i], m[i]) for i in range(tall)]
    lines = []
    for m, diag in zip(mats, diags):
        line = jnp.zeros((8, width), jnp.float32)
        for i in range(tall):
            line = line + jnp.where(eye[8 * i : 8 * i + 8], gathered(m[i], side, 1), 0.0)
        line = jnp.sum(line, axis=0, keepdims=True) * jnp.sqrt(diag)
        lines += [line, pltpu.roll(line, blk, 1)]
    out = jnp.concatenate(lines, axis=0)
    for c in range(out_ref.shape[0]):
        out_ref[c] = out


def fast(*args):
    return fast_inner(*args)


def fast_inner(observed, jacobian, tile_block, params, damping):
    ngx, ngy = lax.axis_size("gx"), lax.axis_size("gy")
    tiles, blk, vox = jacobian.shape
    per = NB // (ngx * ngy)
    half = blk // 2
    pairs = per // 2
    rows = pairs * half
    moved = flipped(observed, ("gx", "gy"), ngx * ngy)
    bits = ngx.bit_length() - 1
    steps = tiles // STEP_TILES
    payload = jax.ShapeDtypeStruct((ngx, rows, vox), jnp.float32)
    extra = jax.ShapeDtypeStruct((ngx, EXTRA, vox), jnp.float32)
    whole = lambda *shape: pl.BlockSpec(shape, lambda s, *_: (0,) * len(shape))
    jspec = pl.BlockSpec((STEP_TILES, blk, vox), lambda s, *_: (s, 0, 0))
    mspec = pl.BlockSpec((STEP_TILES, vox), lambda s, *_: (steps - 1 - s, 0))
    tspec = pl.BlockSpec((STEP_TILES, vox), lambda s, *_: (s, 0))
    calc, keep, send, diag = pl.pallas_call(
        gram_body,
        out_shape=(
            jax.ShapeDtypeStruct((tiles, vox), jnp.float32),
            payload,
            payload,
            jax.ShapeDtypeStruct((2, ngx, pairs, vox), jnp.float32),
        ),
        grid_spec=pltpu.PrefetchScalarGridSpec(
            num_scalar_prefetch=1,
            grid=(steps,),
            in_specs=[jspec, whole(blk, NB)],
            out_specs=(tspec, whole(ngx, rows, vox), whole(ngx, rows, vox), whole(2, ngx, pairs, vox)),
            scratch_shapes=[pltpu.VMEM((NB, blk, 2 * blk), jnp.float32), pltpu.VMEM((blk, NB), jnp.float32)],
        ),
        name="gram",
    )(tile_block, jacobian, params.T)
    mine = keep + xored(send, "gy", 1)
    tied, mine = lax.optimization_barrier((calc, mine))
    got = plane(mine)
    keep, send = pl.pallas_call(
        grad_body,
        out_shape=(extra, extra),
        grid_spec=pltpu.PrefetchScalarGridSpec(
            num_scalar_prefetch=1,
            grid=(steps,),
            in_specs=[jspec, tspec, tspec, mspec, whole(2, ngx, pairs, vox)],
            out_specs=(whole(ngx, EXTRA, vox), whole(ngx, EXTRA, vox)),
            scratch_shapes=[
                pltpu.VMEM((blk, NB), jnp.float32),
                pltpu.VMEM((GROUP, vox), jnp.float32),
                pltpu.VMEM((NB, vox), jnp.float32),
            ],
        ),
        name="grad",
    )(tile_block, jacobian, tied, observed, moved, diag)
    rest = plane(keep + xored(send, "gy", 1))
    both = jnp.concatenate([got, rest], axis=1)
    mine, got = both, jnp.zeros_like(both)
    for s in range(PLANE.bit_length() - 1, bits):
        n = both.shape[0] // 2
        mine, got = both[:n], xored(both[n:], "gx", 1 << s)
        both = mine + got
    smem = pl.BlockSpec(memory_space=pltpu.SMEM)
    vmem = pl.BlockSpec(memory_space=pltpu.VMEM)
    step, misfit = pl.pallas_call(
        solve_body,
        out_shape=(jax.ShapeDtypeStruct((ngx, per, vox), jnp.float32), jax.ShapeDtypeStruct((8, vox), jnp.float32)),
        in_specs=[smem, vmem, vmem],
        out_specs=(vmem, vmem),
        name="solve",
    )(damping, mine[0], got[0])
    every = lax.all_to_all(step, "gx", 0, 0)
    return every.reshape(ngx * per, vox)[:, :blk], misfit[0, 0] / (tiles * ngx * ngy * vox)


def solve_blocks(system, rhs):
    size = system.shape[1]
    augmented = jnp.concatenate([system, rhs[:, :, None]], axis=2)
    augmented = jnp.transpose(augmented, (1, 2, 0))
    row_ids = jnp.arange(size, dtype=jnp.int32)

    def eliminate(step, current):
        column = step.astype(jnp.int32)
        pivot_row = lax.dynamic_index_in_dim(current, column, 0, keepdims=False)
        pivot = lax.dynamic_index_in_dim(pivot_row, column, 0, keepdims=False)
        pivot_row = pivot_row / pivot[None, :]
        factors = lax.dynamic_index_in_dim(current, column, 1, keepdims=False)
        updated = current - factors[:, None, :] * pivot_row[None, :, :]
        is_pivot = (row_ids == column)[:, None, None]
        return jnp.where(is_pivot, pivot_row[None, :, :], updated)

    final = lax.fori_loop(0, size, eliminate, augmented)
    return jnp.transpose(final[:, size, :], (1, 0))


def general(observed, jacobian, tile_block, params, damping):
    ngx, ngy = lax.axis_size("gx"), lax.axis_size("gy")
    moved = flipped(observed, ("gx", "gy"), ngx * ngy)[::-1, ::-1]
    block_ids = jnp.arange(NB, dtype=jnp.int32)
    onehot = (tile_block[:, None] == block_ids[None, :]).astype(jnp.float32)
    tile_params = jnp.dot(onehot, params, precision=lax.Precision.HIGHEST).astype(jnp.bfloat16)
    calc = jnp.einsum("tpv,tp->tv", jacobian, tile_params, preferred_element_type=jnp.float32)
    resid = 0.5 * (observed + moved) - calc
    local_misfit = jnp.sum(resid * resid)
    resid_b = resid.astype(jnp.bfloat16)
    tile_grad = jnp.einsum("tpv,tv->tp", jacobian, resid_b, preferred_element_type=jnp.float32)
    tile_gram = jnp.einsum("tpv,tqv->tpq", jacobian, jacobian, preferred_element_type=jnp.float32)
    gram = jnp.einsum("tb,tpq->bpq", onehot, tile_gram, precision=lax.Precision.HIGHEST)
    grad = jnp.dot(onehot.T, tile_grad, precision=lax.Precision.HIGHEST)
    owned = NB // ngy
    gram, grad, total = lax.psum((gram, grad, local_misfit), ("gx", "gy"))
    first = lax.axis_index("gy") * owned
    gram = lax.dynamic_slice_in_dim(gram, first, owned, 0)
    grad = lax.dynamic_slice_in_dim(grad, first, owned, 0)
    diagonal = jnp.diagonal(gram, axis1=1, axis2=2)
    eye = jnp.eye(gram.shape[1], dtype=jnp.float32)
    system = gram + damping[0] * diagonal[:, :, None] * eye[None] + eye[None]
    delta = solve_blocks(system, grad)
    return delta * jnp.sqrt(diagonal), total / (observed.size * ngx * ngy)


def solution(mesh):
    ngx, ngy = mesh.shape["gx"], mesh.shape["gy"]
    quick = ngy == 2 and ngx > PLANE and ngx & (ngx - 1) == 0 and NB % (2 * ngx * ngy) == 0
    return jax.shard_map(
        fast if quick else general,
        mesh=mesh,
        in_specs=(P(("gx", "gy"), None), P(("gx", "gy"), None, None), P(("gx", "gy")), P(), P()),
        out_specs=(P("gy", None), P()),
        check_vma=False,
    )
```

```python
import jax
import jax.numpy as jnp
from jax import lax
from jax.experimental import pallas as pl
from jax.experimental.pallas import tpu as pltpu
from jax.sharding import PartitionSpec as P

NB = 128
J_PARTS = 4
GROUP = 8
GRAM_UNROLL = 4
GRAD_UNROLL = 8
PACK_UNROLL = 4
PANEL = 8
VMEM_LIMIT = 20 << 20
EXTRA = 8
PLANE = 4


def flipped(value, axes, size):
    return lax.ppermute(value, axes, [(i, size - 1 - i) for i in range(size)])


def xored(value, axis, bit):
    return lax.ppermute(value, axis, [(i, i ^ bit) for i in range(lax.axis_size(axis))])


def plane(value):
    parts = value.reshape(PLANE, value.shape[0] // PLANE, *value.shape[1:])
    total = parts[0]
    for k in range(1, PLANE):
        total = total + xored(parts[k], "gx", k)
    return total


def nt_dot(a, b):
    return lax.dot_general(a, b, (((1,), (1,)), ((), ())), preferred_element_type=jnp.float32)


def gathered(value, index, axis):
    return jnp.take_along_axis(value, index, axis=axis, mode="promise_in_bounds")


def owner_of(c, chunks):
    line = chunks // PLANE
    bits = line.bit_length() - 1
    far = c % line
    swapped = sum(((far >> (bits - 1 - s)) & 1) << s for s in range(bits))
    return (c // line + PLANE * swapped) ^ lax.axis_index("gx")


def first_block(part, c, chunks, per):
    side = lax.axis_index("gy")
    return per * ((side if part == 0 else 1 - side) * chunks + owner_of(c, chunks))


def copies(j_ref, jbuf, sems):
    count = sems.shape[0]
    size = jbuf.shape[1] // count
    parts = []
    for c in range(count):
        rows = pl.ds(c * size, size)
        parts.append(pltpu.make_async_copy(j_ref.at[:, rows], jbuf.at[:, rows], sems.at[c]))
        parts[-1].start()
    return parts, size // GROUP


def diagonal_pair(left, right, zero):
    return jnp.concatenate(
        [jnp.concatenate([left, zero], axis=1), jnp.concatenate([zero, right], axis=1)], axis=0
    )


def gram_body(tb, j_ref, par_ref, calc_ref, keep_ref, send_ref, diag_ref, jbuf, acc, par, sems):
    parts, groups = copies(j_ref, jbuf, sems)
    side_tiles, blk, vox = jbuf.shape[1:]
    half = blk // 2
    acc[...] = jnp.zeros_like(acc)
    par[...] = jnp.concatenate([par_ref[...], par_ref[...]], axis=0).T.astype(jnp.bfloat16).astype(jnp.float32)
    zero = jnp.zeros((blk, vox), jnp.bfloat16)
    low = lax.broadcasted_iota(jnp.int32, (blk, 2 * blk), 1) < blk
    high = jnp.logical_not(low)
    grow = lax.broadcasted_iota(jnp.int32, (GROUP, 2 * blk), 0)
    gside = (lax.broadcasted_iota(jnp.int32, (GROUP, 2 * blk), 1) >= blk).astype(jnp.int32)
    slot = grow - (grow & 1) + gside
    fits = grow == slot

    def group(g, carry):
        base = pl.multiple_of(g * GROUP, GROUP)
        for h in range(2):
            rows = jnp.concatenate(
                [par[pl.ds(tb[h * side_tiles + base + u], 1), :] for u in range(GROUP)], axis=0
            )
            rows = jnp.where(fits, rows, 0.0)
            total = jnp.zeros((GROUP, vox), jnp.float32)
            for a in range(0, GROUP, 4):
                lhs = [jnp.where((grow >= a + v) & (grow < a + v + 2), rows, 0.0) for v in (0, 2)]
                lhs = jnp.concatenate(lhs, axis=1).astype(jnp.bfloat16)
                four = jbuf[h, pl.ds(base + a, 4)].reshape(4 * blk, vox)
                total = total + jnp.dot(lhs, four, preferred_element_type=jnp.float32)
            calc_ref[h, pl.ds(base, GROUP), :] = total
        for u in range(GROUP):
            left, right = jbuf[0, base + u], jbuf[1, base + u]
            gram = nt_dot(jnp.concatenate([left, right], axis=1), diagonal_pair(left, right, zero))
            one, two = tb[base + u], tb[side_tiles + base + u]
            low_sum, high_sum = acc[one] + gram, acc[two] + gram
            pltpu.store(acc.at[one], low_sum, mask=low)
            pltpu.store(acc.at[two], high_sum, mask=high)
        return carry

    for c, part in enumerate(parts):
        part.wait()
        lax.fori_loop(c * groups, (c + 1) * groups, group, 0, unroll=GRAM_UNROLL)

    chunks = keep_ref.shape[0]
    pairs = keep_ref.shape[1] // half
    row = lax.broadcasted_iota(jnp.int32, (half, 2 * blk), 0)
    lane = lax.broadcasted_iota(jnp.int32, (half, 2 * blk), 1) % blk
    use_top = ((lane < half) & (row <= lane)) | ((lane >= half) & (lane - half <= row))
    frow = lax.broadcasted_iota(jnp.int32, (blk, 2 * blk), 0)
    flane = lax.broadcasted_iota(jnp.int32, (blk, 2 * blk), 1) % blk
    on_diag = frow == flane
    for part, ref in enumerate((send_ref, keep_ref)):
        def chunk(c, carry, part=1 - part, ref=ref):
            first = first_block(part, c, chunks, 2 * pairs)
            for p in range(pairs):
                one, two = acc[first + 2 * p], acc[first + 2 * p + 1]
                stay, cross = jnp.where(low, one, two), jnp.where(low, two, one)
                ref[c, p * half : (p + 1) * half, :] = jnp.where(use_top, stay[:half], stay[half:]) + pltpu.roll(
                    jnp.where(use_top, cross[:half], cross[half:]), blk, 1
                )
                lines = [jnp.sum(jnp.where(on_diag, v, 0.0), axis=0, keepdims=True) for v in (stay, cross)]
                diag_ref[part, c, p : p + 1, :] = lines[0] + pltpu.roll(lines[1], blk, 1)
            return carry

        lax.fori_loop(0, chunks, chunk, 0, unroll=PACK_UNROLL)


def grad_body(tb_ref, jbuf, calc_ref, obs_ref, mir_ref, diag_ref, keep_ref, send_ref, tg, mix):
    side_tiles, blk, vox = jbuf.shape[1:]
    tb_rows = tb_ref[...]
    back = vox - 1 - lax.broadcasted_iota(jnp.int32, (GROUP, vox), 1)
    up = GROUP - 1 - lax.broadcasted_iota(jnp.int32, (GROUP, vox), 0)
    sub = lax.broadcasted_iota(jnp.int32, (GROUP, vox), 0)
    zero = jnp.zeros((blk, vox), jnp.bfloat16)

    def group(g, mis):
        base = pl.multiple_of(g * GROUP, GROUP)
        rows = pl.ds(base, GROUP)
        resids = []
        for h in range(2):
            mirror = mir_ref[1 - h, pl.ds(pl.multiple_of(side_tiles - GROUP - base, GROUP), GROUP), :]
            mirror = gathered(gathered(mirror, back, 1), up, 0)
            resid = 0.5 * (obs_ref[h, rows, :] + mirror) - calc_ref[h, rows, :]
            mis = mis + resid * resid
            resids.append(resid)
        lhs = jnp.concatenate(resids, axis=1).astype(jnp.bfloat16)
        lines = jnp.zeros((GROUP, vox), jnp.float32)
        for u in range(GROUP):
            grad = nt_dot(lhs, diagonal_pair(jbuf[0, base + u], jbuf[1, base + u], zero))
            lines = jnp.where(sub == u, grad, lines)
        tg[rows, :] = lines
        return mis

    mis = lax.fori_loop(0, side_tiles // GROUP, group, jnp.zeros((GROUP, vox), jnp.float32), unroll=GRAD_UNROLL)

    chunks = keep_ref.shape[0]
    pairs = diag_ref.shape[2]
    total = jnp.sum(mis, axis=0, keepdims=True)
    rest = jnp.zeros((EXTRA - 2 * pairs - 1, vox), jnp.float32)
    block = lax.broadcasted_iota(jnp.int32, (NB, side_tiles), 0)
    sums = [
        jnp.dot(
            (block == tb_row).astype(jnp.float32),
            tg[...],
            precision=lax.Precision.HIGHEST,
            preferred_element_type=jnp.float32,
        )
        for tb_row in (tb_rows[0:1], tb_rows[1:2])
    ]
    high = lax.broadcasted_iota(jnp.int32, sums[0].shape, 1) >= blk
    odd = (lax.broadcasted_iota(jnp.int32, sums[0].shape, 0) % 2) == 1
    own = jnp.where(high, sums[1], sums[0])
    mix[...] = jnp.where(odd == high, own + pltpu.roll(own, blk, 1), 0.0)
    for part, ref in enumerate((keep_ref, send_ref)):
        def chunk(c, carry, part=part, ref=ref):
            first = first_block(part, c, chunks, 2 * pairs)
            rows = [mix[pl.ds(first + 2 * p, 1), :] + mix[pl.ds(first + 2 * p + 1, 1), :] for p in range(pairs)]
            ref[c] = jnp.concatenate(rows + [diag_ref[part, c], total, rest], axis=0)
            return carry

        lax.fori_loop(0, chunks, chunk, 0, unroll=PACK_UNROLL)


def solve_body(damp, a_ref, b_ref, out_ref, mis_ref):
    x = a_ref[0] + b_ref[0]
    width = x.shape[1]
    blk = width // 2
    half = blk // 2
    tall = blk // 8
    pairs = (x.shape[0] - EXTRA) // half
    ext = x[pairs * half :]
    mis_ref[...] = jnp.broadcast_to(jnp.sum(ext[2 * pairs : 2 * pairs + 1], axis=1, keepdims=True), mis_ref.shape)
    row = lax.broadcasted_iota(jnp.int32, (half, width), 0)
    lane = lax.broadcasted_iota(jnp.int32, (half, width), 1)
    inner = lane % blk
    frow = lax.broadcasted_iota(jnp.int32, (blk, width), 0)
    flane = lax.broadcasted_iota(jnp.int32, (blk, width), 1)
    eye = frow == flane % blk
    scale = damp[0]
    mats = []
    rights = []
    diags = []
    for p in range(pairs):
        t = x[p * half : (p + 1) * half]
        grad = ext[p : p + 1]
        diag = ext[pairs + p : pairs + p + 1]
        tt = jnp.concatenate([t, jnp.zeros((width - half, width), jnp.float32)], axis=0).T
        mt = jnp.where(lane < blk, tt[:half], pltpu.roll(tt[blk : blk + half], blk, 1))
        bt = jnp.where(lane < blk, tt[half:blk], pltpu.roll(tt[blk + half :], blk, 1))
        top = jnp.where(
            inner < half,
            jnp.where(row <= inner, t, mt),
            jnp.where(inner - half <= row, t, pltpu.roll(mt, half, 1)),
        )
        bot = jnp.where(
            inner < half,
            jnp.where(row > inner, t, bt),
            jnp.where(inner - half > row, t, pltpu.roll(bt, half, 1)),
        )
        full = jnp.concatenate([top, bot], axis=0)
        full = jnp.where(eye, (diag + scale * diag) + 1.0, full)
        cols = jnp.where(eye, jnp.broadcast_to(grad, (blk, width)), 0.0)
        right = jnp.where(
            flane < blk,
            jnp.sum(jnp.where(flane < blk, cols, 0.0), axis=1, keepdims=True),
            jnp.sum(jnp.where(flane < blk, 0.0, cols), axis=1, keepdims=True),
        )
        mats.append([full[8 * i : 8 * i + 8] for i in range(tall)])
        rights.append([right[8 * i : 8 * i + 8] for i in range(tall)])
        diags.append(diag)
    sub = lax.broadcasted_iota(jnp.int32, (8, width), 0)
    lanes = lax.broadcasted_iota(jnp.int32, (8, width), 1)
    side = lanes - lanes % blk
    for k in range(0, blk, PANEL):
        own = k // 8
        for m, right in zip(mats, rights):
            cols = [[gathered(m[i], side + (k + j), 1) for i in range(tall)] for j in range(PANEL)]
            if k == 0:
                cols.append(right)
            for j in range(PANEL):
                at = (k + j) % 8
                pivot = jnp.broadcast_to(cols[j][own][at : at + 1], (8, width))

                def eliminate(part):
                    prow = jnp.broadcast_to(part[own][at : at + 1], (8, width)) / pivot
                    new = [part[i] - cols[j][i] * prow for i in range(tall)]
                    new[own] = jnp.where(sub == at, prow, new[own])
                    return new

                cols[j + 1 :] = [eliminate(col) for col in cols[j + 1 :]]
                m[:] = eliminate(m)
            if k == 0:
                m[:] = [jnp.where(lanes == side, cols[PANEL][i], m[i]) for i in range(tall)]
    lines = []
    for m, diag in zip(mats, diags):
        line = jnp.zeros((8, width), jnp.float32)
        for i in range(tall):
            line = line + jnp.where(eye[8 * i : 8 * i + 8], gathered(m[i], side, 1), 0.0)
        line = jnp.sum(line, axis=0, keepdims=True) * jnp.sqrt(diag)
        lines += [line, pltpu.roll(line, blk, 1)]
    out = jnp.concatenate(lines, axis=0)
    for c in range(out_ref.shape[0]):
        out_ref[c] = out


def fast(*args):
    return fast_inner(*args)


def fast_inner(observed, jacobian, tile_block, params, damping):
    ngx, ngy = lax.axis_size("gx"), lax.axis_size("gy")
    tiles, blk, vox = jacobian.shape
    per = NB // (ngx * ngy)
    half = blk // 2
    pairs = per // 2
    rows = pairs * half
    moved = flipped(observed, ("gx", "gy"), ngx * ngy)
    bits = ngx.bit_length() - 1
    side_tiles = tiles // 2
    local = lambda value: pltpu.with_memory_space_constraint(value, pltpu.VMEM)
    limit = pltpu.CompilerParams(vmem_limit_bytes=VMEM_LIMIT)
    halved = lambda value: value.reshape(2, side_tiles, *value.shape[1:])
    payload = pltpu.VMEM((ngx, rows, vox), jnp.float32)
    extra = pltpu.VMEM((ngx, EXTRA, vox), jnp.float32)
    smem = pl.BlockSpec(memory_space=pltpu.SMEM)
    vmem = pl.BlockSpec(memory_space=pltpu.VMEM)
    hbm = pl.BlockSpec(memory_space=pl.ANY)
    far = lambda value: pltpu.with_memory_space_constraint(value, pltpu.HBM)
    calc, keep, send, diag, staged = pl.pallas_call(
        gram_body,
        out_shape=(
            pltpu.VMEM((2, side_tiles, vox), jnp.float32),
            payload,
            payload,
            pltpu.VMEM((2, ngx, pairs, vox), jnp.float32),
            pltpu.VMEM((2, side_tiles, blk, vox), jnp.bfloat16),
        ),
        in_specs=[smem, hbm, vmem],
        out_specs=(vmem, vmem, vmem, vmem, vmem),
        scratch_shapes=[
            pltpu.VMEM((NB, blk, 2 * blk), jnp.float32),
            pltpu.VMEM((NB, 2 * blk), jnp.float32),
            pltpu.SemaphoreType.DMA((J_PARTS,)),
        ],
        compiler_params=limit,
        name="gram",
    )(far(tile_block), far(halved(jacobian)), far(params.T))
    mine = keep + xored(send, "gy", 1)
    tied, mine = lax.optimization_barrier((calc, mine))
    got = plane(mine)
    keep, send = pl.pallas_call(
        grad_body,
        out_shape=(extra, extra),
        in_specs=[vmem] * 6,
        out_specs=(vmem, vmem),
        scratch_shapes=[pltpu.VMEM((side_tiles, vox), jnp.float32), pltpu.VMEM((NB, vox), jnp.float32)],
        compiler_params=limit,
        name="grad",
    )(halved(tile_block), local(staged), local(tied), halved(observed), local(halved(moved)), local(diag))
    rest = plane(keep + xored(send, "gy", 1))
    both = jnp.concatenate([got, rest], axis=1)
    mine, got = both, jnp.zeros_like(both)
    for s in range(PLANE.bit_length() - 1, bits):
        n = both.shape[0] // 2
        mine, got = both[:n], xored(both[n:], "gx", 1 << s)
        both = mine + got
    step, misfit = pl.pallas_call(
        solve_body,
        out_shape=(jax.ShapeDtypeStruct((ngx, per, vox), jnp.float32), jax.ShapeDtypeStruct((8, vox), jnp.float32)),
        in_specs=[smem, vmem, vmem],
        out_specs=(vmem, vmem),
        compiler_params=limit,
        name="solve",
    )(damping, local(mine), local(got))
    every = lax.all_to_all(step, "gx", 0, 0)
    return every.reshape(ngx * per, vox)[:, :blk], misfit[0, 0] / (tiles * ngx * ngy * vox)


def solve_blocks(system, rhs):
    size = system.shape[1]
    augmented = jnp.concatenate([system, rhs[:, :, None]], axis=2)
    augmented = jnp.transpose(augmented, (1, 2, 0))
    row_ids = jnp.arange(size, dtype=jnp.int32)

    def eliminate(step, current):
        column = step.astype(jnp.int32)
        pivot_row = lax.dynamic_index_in_dim(current, column, 0, keepdims=False)
        pivot = lax.dynamic_index_in_dim(pivot_row, column, 0, keepdims=False)
        pivot_row = pivot_row / pivot[None, :]
        factors = lax.dynamic_index_in_dim(current, column, 1, keepdims=False)
        updated = current - factors[:, None, :] * pivot_row[None, :, :]
        is_pivot = (row_ids == column)[:, None, None]
        return jnp.where(is_pivot, pivot_row[None, :, :], updated)

    final = lax.fori_loop(0, size, eliminate, augmented)
    return jnp.transpose(final[:, size, :], (1, 0))


def general(observed, jacobian, tile_block, params, damping):
    ngx, ngy = lax.axis_size("gx"), lax.axis_size("gy")
    moved = flipped(observed, ("gx", "gy"), ngx * ngy)[::-1, ::-1]
    block_ids = jnp.arange(NB, dtype=jnp.int32)
    onehot = (tile_block[:, None] == block_ids[None, :]).astype(jnp.float32)
    tile_params = jnp.dot(onehot, params, precision=lax.Precision.HIGHEST).astype(jnp.bfloat16)
    calc = jnp.einsum("tpv,tp->tv", jacobian, tile_params, preferred_element_type=jnp.float32)
    resid = 0.5 * (observed + moved) - calc
    local_misfit = jnp.sum(resid * resid)
    resid_b = resid.astype(jnp.bfloat16)
    tile_grad = jnp.einsum("tpv,tv->tp", jacobian, resid_b, preferred_element_type=jnp.float32)
    tile_gram = jnp.einsum("tpv,tqv->tpq", jacobian, jacobian, preferred_element_type=jnp.float32)
    gram = jnp.einsum("tb,tpq->bpq", onehot, tile_gram, precision=lax.Precision.HIGHEST)
    grad = jnp.dot(onehot.T, tile_grad, precision=lax.Precision.HIGHEST)
    owned = NB // ngy
    gram, grad, total = lax.psum((gram, grad, local_misfit), ("gx", "gy"))
    first = lax.axis_index("gy") * owned
    gram = lax.dynamic_slice_in_dim(gram, first, owned, 0)
    grad = lax.dynamic_slice_in_dim(grad, first, owned, 0)
    diagonal = jnp.diagonal(gram, axis1=1, axis2=2)
    eye = jnp.eye(gram.shape[1], dtype=jnp.float32)
    system = gram + damping[0] * diagonal[:, :, None] * eye[None] + eye[None]
    delta = solve_blocks(system, grad)
    return delta * jnp.sqrt(diagonal), total / (observed.size * ngx * ngy)


def solution(mesh):
    ngx, ngy = mesh.shape["gx"], mesh.shape["gy"]
    quick = ngy == 2 and ngx > PLANE and ngx & (ngx - 1) == 0 and NB % (2 * ngx * ngy) == 0
    return jax.shard_map(
        fast if quick else general,
        mesh=mesh,
        in_specs=(P(("gx", "gy"), None), P(("gx", "gy"), None, None), P(("gx", "gy")), P(), P()),
        out_specs=(P("gy", None), P()),
        check_vma=False,
    )
```

```python
import jax
import jax.numpy as jnp
from jax import lax
from jax.experimental import pallas as pl
from jax.experimental.pallas import tpu as pltpu
from jax.sharding import PartitionSpec as P

NB = 128
J_PARTS = 4
GROUP = 8
GRAM_UNROLL = 4
GRAD_UNROLL = 8
PACK_UNROLL = 4
PANEL = 8
VMEM_LIMIT = 20 << 20
EXTRA = 8
PLANE = 4


def flipped(value, axes, size):
    return lax.ppermute(value, axes, [(i, size - 1 - i) for i in range(size)])


def xored(value, axis, bit):
    return lax.ppermute(value, axis, [(i, i ^ bit) for i in range(lax.axis_size(axis))])


def plane(value):
    parts = value.reshape(PLANE, value.shape[0] // PLANE, *value.shape[1:])
    total = parts[0]
    for k in range(1, PLANE):
        total = total + xored(parts[k], "gx", k)
    return total


def nt_dot(a, b):
    return lax.dot_general(a, b, (((1,), (1,)), ((), ())), preferred_element_type=jnp.float32)


def gathered(value, index, axis):
    return jnp.take_along_axis(value, index, axis=axis, mode="promise_in_bounds")


def owner_of(c, chunks):
    line = chunks // PLANE
    bits = line.bit_length() - 1
    far = c % line
    swapped = sum(((far >> (bits - 1 - s)) & 1) << s for s in range(bits))
    return (c // line + PLANE * swapped) ^ lax.axis_index("gx")


def first_block(part, c, chunks, per):
    side = lax.axis_index("gy")
    return per * ((side if part == 0 else 1 - side) * chunks + owner_of(c, chunks))


def copies(j_ref, jbuf, sems):
    count = sems.shape[0]
    size = jbuf.shape[1] // count
    parts = []
    for c in range(count):
        rows = pl.ds(c * size, size)
        parts.append(pltpu.make_async_copy(j_ref.at[:, rows], jbuf.at[:, rows], sems.at[c]))
        parts[-1].start()
    return parts, size // GROUP


def diagonal_pair(left, right, zero):
    return jnp.concatenate(
        [jnp.concatenate([left, zero], axis=1), jnp.concatenate([zero, right], axis=1)], axis=0
    )


def gram_body(tb, j_ref, par_ref, calc_ref, keep_ref, send_ref, diag_ref, jbuf, acc, par, sems):
    parts, groups = copies(j_ref, jbuf, sems)
    side_tiles, blk, vox = jbuf.shape[1:]
    half = blk // 2
    acc[...] = jnp.zeros_like(acc)
    par[...] = jnp.concatenate([par_ref[...], par_ref[...]], axis=0).T.astype(jnp.bfloat16).astype(jnp.float32)
    zero = jnp.zeros((blk, vox), jnp.bfloat16)
    low = lax.broadcasted_iota(jnp.int32, (blk, 2 * blk), 1) < blk
    high = jnp.logical_not(low)
    grow = lax.broadcasted_iota(jnp.int32, (GROUP, 2 * blk), 0)
    gside = (lax.broadcasted_iota(jnp.int32, (GROUP, 2 * blk), 1) >= blk).astype(jnp.int32)
    slot = grow - (grow & 1) + gside
    fits = grow == slot

    def group(g, carry):
        base = pl.multiple_of(g * GROUP, GROUP)
        for h in range(2):
            rows = jnp.concatenate(
                [par[pl.ds(tb[h * side_tiles + base + u], 1), :] for u in range(GROUP)], axis=0
            )
            rows = jnp.where(fits, rows, 0.0)
            total = jnp.zeros((GROUP, vox), jnp.float32)
            for a in range(0, GROUP, 4):
                lhs = [jnp.where((grow >= a + v) & (grow < a + v + 2), rows, 0.0) for v in (0, 2)]
                lhs = jnp.concatenate(lhs, axis=1).astype(jnp.bfloat16)
                four = jbuf[h, pl.ds(base + a, 4)].reshape(4 * blk, vox)
                total = total + jnp.dot(lhs, four, preferred_element_type=jnp.float32)
            calc_ref[h, pl.ds(base, GROUP), :] = total
        for u in range(GROUP):
            left, right = jbuf[0, base + u], jbuf[1, base + u]
            gram = nt_dot(jnp.concatenate([left, right], axis=1), diagonal_pair(left, right, zero))
            one, two = tb[base + u], tb[side_tiles + base + u]
            low_sum, high_sum = acc[one] + gram, acc[two] + gram
            pltpu.store(acc.at[one], low_sum, mask=low)
            pltpu.store(acc.at[two], high_sum, mask=high)
        return carry

    for c, part in enumerate(parts):
        part.wait()
        lax.fori_loop(c * groups, (c + 1) * groups, group, 0, unroll=GRAM_UNROLL)

    chunks = keep_ref.shape[0]
    pairs = keep_ref.shape[1] // half
    row = lax.broadcasted_iota(jnp.int32, (half, 2 * blk), 0)
    lane = lax.broadcasted_iota(jnp.int32, (half, 2 * blk), 1) % blk
    use_top = ((lane < half) & (row <= lane)) | ((lane >= half) & (lane - half <= row))
    frow = lax.broadcasted_iota(jnp.int32, (blk, 2 * blk), 0)
    flane = lax.broadcasted_iota(jnp.int32, (blk, 2 * blk), 1) % blk
    on_diag = frow == flane
    for part, ref in enumerate((send_ref, keep_ref)):
        def chunk(c, carry, part=1 - part, ref=ref):
            first = first_block(part, c, chunks, 2 * pairs)
            for p in range(pairs):
                one, two = acc[first + 2 * p], acc[first + 2 * p + 1]
                stay, cross = jnp.where(low, one, two), jnp.where(low, two, one)
                ref[c, p * half : (p + 1) * half, :] = jnp.where(use_top, stay[:half], stay[half:]) + pltpu.roll(
                    jnp.where(use_top, cross[:half], cross[half:]), blk, 1
                )
                lines = [jnp.sum(jnp.where(on_diag, v, 0.0), axis=0, keepdims=True) for v in (stay, cross)]
                diag_ref[part, c, p : p + 1, :] = lines[0] + pltpu.roll(lines[1], blk, 1)
            return carry

        lax.fori_loop(0, chunks, chunk, 0, unroll=PACK_UNROLL)


def grad_body(tb_ref, jbuf, calc_ref, obs_ref, mir_ref, diag_ref, keep_ref, send_ref, tg, mix):
    side_tiles, blk, vox = jbuf.shape[1:]
    tb_rows = tb_ref[...]
    back = vox - 1 - lax.broadcasted_iota(jnp.int32, (GROUP, vox), 1)
    up = GROUP - 1 - lax.broadcasted_iota(jnp.int32, (GROUP, vox), 0)
    sub = lax.broadcasted_iota(jnp.int32, (GROUP, vox), 0)
    zero = jnp.zeros((blk, vox), jnp.bfloat16)

    def group(g, mis):
        base = pl.multiple_of(g * GROUP, GROUP)
        rows = pl.ds(base, GROUP)
        resids = []
        for h in range(2):
            mirror = mir_ref[1 - h, pl.ds(pl.multiple_of(side_tiles - GROUP - base, GROUP), GROUP), :]
            mirror = gathered(gathered(mirror, back, 1), up, 0)
            resid = 0.5 * (obs_ref[h, rows, :] + mirror) - calc_ref[h, rows, :]
            mis = mis + resid * resid
            resids.append(resid)
        lhs = jnp.concatenate(resids, axis=1).astype(jnp.bfloat16)
        lines = jnp.zeros((GROUP, vox), jnp.float32)
        for u in range(GROUP):
            grad = nt_dot(lhs, diagonal_pair(jbuf[0, base + u], jbuf[1, base + u], zero))
            lines = jnp.where(sub == u, grad, lines)
        tg[rows, :] = lines
        return mis

    mis = lax.fori_loop(0, side_tiles // GROUP, group, jnp.zeros((GROUP, vox), jnp.float32), unroll=GRAD_UNROLL)

    chunks = keep_ref.shape[0]
    pairs = diag_ref.shape[2]
    total = jnp.sum(mis, axis=0, keepdims=True)
    rest = jnp.zeros((EXTRA - 2 * pairs - 1, vox), jnp.float32)
    block = lax.broadcasted_iota(jnp.int32, (NB, side_tiles), 0)
    sums = [
        jnp.dot(
            (block == tb_row).astype(jnp.float32),
            tg[...],
            precision=lax.Precision.HIGHEST,
            preferred_element_type=jnp.float32,
        )
        for tb_row in (tb_rows[0:1], tb_rows[1:2])
    ]
    high = lax.broadcasted_iota(jnp.int32, sums[0].shape, 1) >= blk
    odd = (lax.broadcasted_iota(jnp.int32, sums[0].shape, 0) % 2) == 1
    own = jnp.where(high, sums[1], sums[0])
    mix[...] = jnp.where(odd == high, own + pltpu.roll(own, blk, 1), 0.0)
    for part, ref in enumerate((keep_ref, send_ref)):
        def chunk(c, carry, part=part, ref=ref):
            first = first_block(part, c, chunks, 2 * pairs)
            rows = [mix[pl.ds(first + 2 * p, 1), :] + mix[pl.ds(first + 2 * p + 1, 1), :] for p in range(pairs)]
            ref[c] = jnp.concatenate(rows + [diag_ref[part, c], total, rest], axis=0)
            return carry

        lax.fori_loop(0, chunks, chunk, 0, unroll=PACK_UNROLL)


def solve_body(damp, a_ref, b_ref, out_ref, mis_ref):
    x = a_ref[0] + b_ref[0]
    width = x.shape[1]
    blk = width // 2
    half = blk // 2
    tall = blk // 8
    pairs = (x.shape[0] - EXTRA) // half
    ext = x[pairs * half :]
    mis_ref[...] = jnp.broadcast_to(jnp.sum(ext[2 * pairs : 2 * pairs + 1], axis=1, keepdims=True), mis_ref.shape)
    row = lax.broadcasted_iota(jnp.int32, (half, width), 0)
    lane = lax.broadcasted_iota(jnp.int32, (half, width), 1)
    inner = lane % blk
    frow = lax.broadcasted_iota(jnp.int32, (blk, width), 0)
    flane = lax.broadcasted_iota(jnp.int32, (blk, width), 1)
    eye = frow == flane % blk
    scale = damp[0]
    mats = []
    rights = []
    diags = []
    for p in range(pairs):
        t = x[p * half : (p + 1) * half]
        grad = ext[p : p + 1]
        diag = ext[pairs + p : pairs + p + 1]
        tt = jnp.concatenate([t, jnp.zeros((width - half, width), jnp.float32)], axis=0).T
        mt = jnp.where(lane < blk, tt[:half], pltpu.roll(tt[blk : blk + half], blk, 1))
        bt = jnp.where(lane < blk, tt[half:blk], pltpu.roll(tt[blk + half :], blk, 1))
        top = jnp.where(
            inner < half,
            jnp.where(row <= inner, t, mt),
            jnp.where(inner - half <= row, t, pltpu.roll(mt, half, 1)),
        )
        bot = jnp.where(
            inner < half,
            jnp.where(row > inner, t, bt),
            jnp.where(inner - half > row, t, pltpu.roll(bt, half, 1)),
        )
        full = jnp.concatenate([top, bot], axis=0)
        full = jnp.where(eye, (diag + scale * diag) + 1.0, full)
        cols = jnp.where(eye, jnp.broadcast_to(grad, (blk, width)), 0.0)
        right = jnp.where(
            flane < blk,
            jnp.sum(jnp.where(flane < blk, cols, 0.0), axis=1, keepdims=True),
            jnp.sum(jnp.where(flane < blk, 0.0, cols), axis=1, keepdims=True),
        )
        mats.append([full[8 * i : 8 * i + 8] for i in range(tall)])
        rights.append([right[8 * i : 8 * i + 8] for i in range(tall)])
        diags.append(diag)
    sub = lax.broadcasted_iota(jnp.int32, (8, width), 0)
    lanes = lax.broadcasted_iota(jnp.int32, (8, width), 1)
    side = lanes - lanes % blk
    for k in range(0, blk, PANEL):
        own = k // 8
        for m, right in zip(mats, rights):
            cols = [[gathered(m[i], side + (k + j), 1) for i in range(tall)] for j in range(PANEL)]
            if k == 0:
                cols.append(right)
            for j in range(PANEL):
                at = (k + j) % 8
                pivot = jnp.broadcast_to(cols[j][own][at : at + 1], (8, width))

                def eliminate(part):
                    prow = jnp.broadcast_to(part[own][at : at + 1], (8, width)) / pivot
                    new = [part[i] - cols[j][i] * prow for i in range(tall)]
                    new[own] = jnp.where(sub == at, prow, new[own])
                    return new

                cols[j + 1 :] = [eliminate(col) for col in cols[j + 1 :]]
                m[:] = eliminate(m)
            if k == 0:
                m[:] = [jnp.where(lanes == side, cols[PANEL][i], m[i]) for i in range(tall)]
    lines = []
    for m, diag in zip(mats, diags):
        line = jnp.zeros((8, width), jnp.float32)
        for i in range(tall):
            line = line + jnp.where(eye[8 * i : 8 * i + 8], gathered(m[i], side, 1), 0.0)
        line = jnp.sum(line, axis=0, keepdims=True) * jnp.sqrt(diag)
        lines += [line, pltpu.roll(line, blk, 1)]
    out = jnp.concatenate(lines, axis=0)
    for c in range(out_ref.shape[0]):
        out_ref[c] = out


def fast(*args):
    return fast_inner(*args)


def fast_inner(observed, jacobian, tile_block, params, damping):
    ngx, ngy = lax.axis_size("gx"), lax.axis_size("gy")
    tiles, blk, vox = jacobian.shape
    per = NB // (ngx * ngy)
    half = blk // 2
    pairs = per // 2
    rows = pairs * half
    moved = flipped(observed, ("gx", "gy"), ngx * ngy)
    bits = ngx.bit_length() - 1
    side_tiles = tiles // 2
    local = lambda value: pltpu.with_memory_space_constraint(value, pltpu.VMEM)
    limit = pltpu.CompilerParams(vmem_limit_bytes=VMEM_LIMIT)
    halved = lambda value: value.reshape(2, side_tiles, *value.shape[1:])
    payload = pltpu.VMEM((ngx, rows, vox), jnp.float32)
    extra = pltpu.VMEM((ngx, EXTRA, vox), jnp.float32)
    smem = pl.BlockSpec(memory_space=pltpu.SMEM)
    vmem = pl.BlockSpec(memory_space=pltpu.VMEM)
    hbm = pl.BlockSpec(memory_space=pl.ANY)
    far = lambda value: pltpu.with_memory_space_constraint(value, pltpu.HBM)
    calc, keep, send, diag, staged = pl.pallas_call(
        gram_body,
        out_shape=(
            pltpu.VMEM((2, side_tiles, vox), jnp.float32),
            payload,
            payload,
            pltpu.VMEM((2, ngx, pairs, vox), jnp.float32),
            pltpu.VMEM((2, side_tiles, blk, vox), jnp.bfloat16),
        ),
        in_specs=[smem, hbm, vmem],
        out_specs=(vmem, vmem, vmem, vmem, vmem),
        scratch_shapes=[
            pltpu.VMEM((NB, blk, 2 * blk), jnp.float32),
            pltpu.VMEM((NB, 2 * blk), jnp.float32),
            pltpu.SemaphoreType.DMA((J_PARTS,)),
        ],
        compiler_params=limit,
        name="gram",
    )(far(tile_block), far(halved(jacobian)), far(params.T))
    other = xored(send, "gy", 1)
    got = plane(keep + other)
    keep, send = pl.pallas_call(
        grad_body,
        out_shape=(extra, extra),
        in_specs=[vmem] * 6,
        out_specs=(vmem, vmem),
        scratch_shapes=[pltpu.VMEM((side_tiles, vox), jnp.float32), pltpu.VMEM((NB, vox), jnp.float32)],
        compiler_params=limit,
        name="grad",
    )(halved(tile_block), local(staged), local(calc), halved(observed), local(halved(moved)), local(diag))
    other = xored(send, "gy", 1)
    both = keep + other
    rest = plane(both)
    both = jnp.concatenate([got, rest], axis=1)
    mine, got = both, jnp.zeros_like(both)
    for s in range(PLANE.bit_length() - 1, bits):
        n = both.shape[0] // 2
        mine, got = both[:n], xored(both[n:], "gx", 1 << s)
        both = mine + got
    step, misfit = pl.pallas_call(
        solve_body,
        out_shape=(jax.ShapeDtypeStruct((ngx, per, vox), jnp.float32), jax.ShapeDtypeStruct((8, vox), jnp.float32)),
        in_specs=[smem, vmem, vmem],
        out_specs=(vmem, vmem),
        compiler_params=limit,
        name="solve",
    )(damping, local(mine), local(got))
    every = lax.all_to_all(step, "gx", 0, 0)
    return every.reshape(ngx * per, vox)[:, :blk], misfit[0, 0] / (tiles * ngx * ngy * vox)


def solve_blocks(system, rhs):
    size = system.shape[1]
    augmented = jnp.concatenate([system, rhs[:, :, None]], axis=2)
    augmented = jnp.transpose(augmented, (1, 2, 0))
    row_ids = jnp.arange(size, dtype=jnp.int32)

    def eliminate(step, current):
        column = step.astype(jnp.int32)
        pivot_row = lax.dynamic_index_in_dim(current, column, 0, keepdims=False)
        pivot = lax.dynamic_index_in_dim(pivot_row, column, 0, keepdims=False)
        pivot_row = pivot_row / pivot[None, :]
        factors = lax.dynamic_index_in_dim(current, column, 1, keepdims=False)
        updated = current - factors[:, None, :] * pivot_row[None, :, :]
        is_pivot = (row_ids == column)[:, None, None]
        return jnp.where(is_pivot, pivot_row[None, :, :], updated)

    final = lax.fori_loop(0, size, eliminate, augmented)
    return jnp.transpose(final[:, size, :], (1, 0))


def general(observed, jacobian, tile_block, params, damping):
    ngx, ngy = lax.axis_size("gx"), lax.axis_size("gy")
    moved = flipped(observed, ("gx", "gy"), ngx * ngy)[::-1, ::-1]
    block_ids = jnp.arange(NB, dtype=jnp.int32)
    onehot = (tile_block[:, None] == block_ids[None, :]).astype(jnp.float32)
    tile_params = jnp.dot(onehot, params, precision=lax.Precision.HIGHEST).astype(jnp.bfloat16)
    calc = jnp.einsum("tpv,tp->tv", jacobian, tile_params, preferred_element_type=jnp.float32)
    resid = 0.5 * (observed + moved) - calc
    local_misfit = jnp.sum(resid * resid)
    resid_b = resid.astype(jnp.bfloat16)
    tile_grad = jnp.einsum("tpv,tv->tp", jacobian, resid_b, preferred_element_type=jnp.float32)
    tile_gram = jnp.einsum("tpv,tqv->tpq", jacobian, jacobian, preferred_element_type=jnp.float32)
    gram = jnp.einsum("tb,tpq->bpq", onehot, tile_gram, precision=lax.Precision.HIGHEST)
    grad = jnp.dot(onehot.T, tile_grad, precision=lax.Precision.HIGHEST)
    owned = NB // ngy
    gram, grad, total = lax.psum((gram, grad, local_misfit), ("gx", "gy"))
    first = lax.axis_index("gy") * owned
    gram = lax.dynamic_slice_in_dim(gram, first, owned, 0)
    grad = lax.dynamic_slice_in_dim(grad, first, owned, 0)
    diagonal = jnp.diagonal(gram, axis1=1, axis2=2)
    eye = jnp.eye(gram.shape[1], dtype=jnp.float32)
    system = gram + damping[0] * diagonal[:, :, None] * eye[None] + eye[None]
    delta = solve_blocks(system, grad)
    return delta * jnp.sqrt(diagonal), total / (observed.size * ngx * ngy)


def solution(mesh):
    ngx, ngy = mesh.shape["gx"], mesh.shape["gy"]
    quick = ngy == 2 and ngx > PLANE and ngx & (ngx - 1) == 0 and NB % (2 * ngx * ngy) == 0
    return jax.shard_map(
        fast if quick else general,
        mesh=mesh,
        in_specs=(P(("gx", "gy"), None), P(("gx", "gy"), None, None), P(("gx", "gy")), P(), P()),
        out_specs=(P("gy", None), P()),
        check_vma=False,
    )
```

```python
import jax
import jax.numpy as jnp
from jax import lax
from jax.experimental import pallas as pl
from jax.experimental.pallas import tpu as pltpu
from jax.sharding import PartitionSpec as P

NB = 128
J_PARTS = 4
GROUP = 8
GRAM_UNROLL = 4
GRAD_UNROLL = 8
PACK_UNROLL = 4
VMEM_LIMIT = 20 << 20
EXTRA = 8
PLANE = 4


def flipped(value, axes, size):
    return lax.ppermute(value, axes, [(i, size - 1 - i) for i in range(size)])


def xored(value, axis, bit):
    return lax.ppermute(value, axis, [(i, i ^ bit) for i in range(lax.axis_size(axis))])


def plane(value):
    parts = value.reshape(PLANE, value.shape[0] // PLANE, *value.shape[1:])
    total = parts[0]
    for k in range(1, PLANE):
        total = total + xored(parts[k], "gx", k)
    return total


def nt_dot(a, b):
    return lax.dot_general(a, b, (((1,), (1,)), ((), ())), preferred_element_type=jnp.float32)


def gathered(value, index, axis):
    return jnp.take_along_axis(value, index, axis=axis, mode="promise_in_bounds")


def owner_of(c, chunks):
    line = chunks // PLANE
    bits = line.bit_length() - 1
    far = c % line
    swapped = sum(((far >> (bits - 1 - s)) & 1) << s for s in range(bits))
    return (c // line + PLANE * swapped) ^ lax.axis_index("gx")


def first_block(part, c, chunks, per):
    side = lax.axis_index("gy")
    return per * ((side if part == 0 else 1 - side) * chunks + owner_of(c, chunks))


def copies(j_ref, jbuf, sems):
    count = sems.shape[0]
    size = jbuf.shape[1] // count
    parts = []
    for c in range(count):
        rows = pl.ds(c * size, size)
        parts.append(pltpu.make_async_copy(j_ref.at[:, rows], jbuf.at[:, rows], sems.at[c]))
        parts[-1].start()
    return parts, size // GROUP


def diagonal_pair(left, right, zero):
    return jnp.concatenate(
        [jnp.concatenate([left, zero], axis=1), jnp.concatenate([zero, right], axis=1)], axis=0
    )


def gram_body(tb, j_ref, par_ref, calc_ref, keep_ref, send_ref, diag_ref, jbuf, acc, par, sems):
    parts, groups = copies(j_ref, jbuf, sems)
    side_tiles, blk, vox = jbuf.shape[1:]
    half = blk // 2
    acc[...] = jnp.zeros_like(acc)
    par[...] = jnp.concatenate([par_ref[...], par_ref[...]], axis=0).T.astype(jnp.bfloat16).astype(jnp.float32)
    zero = jnp.zeros((blk, vox), jnp.bfloat16)
    low = lax.broadcasted_iota(jnp.int32, (blk, 2 * blk), 1) < blk
    high = jnp.logical_not(low)
    grow = lax.broadcasted_iota(jnp.int32, (GROUP, 2 * blk), 0)
    gside = (lax.broadcasted_iota(jnp.int32, (GROUP, 2 * blk), 1) >= blk).astype(jnp.int32)
    slot = grow - (grow & 1) + gside
    fits = grow == slot

    def group(g, carry):
        base = pl.multiple_of(g * GROUP, GROUP)
        for h in range(2):
            rows = jnp.concatenate(
                [par[pl.ds(tb[h * side_tiles + base + u], 1), :] for u in range(GROUP)], axis=0
            )
            rows = jnp.where(fits, rows, 0.0)
            total = jnp.zeros((GROUP, vox), jnp.float32)
            for a in range(0, GROUP, 4):
                lhs = [jnp.where((grow >= a + v) & (grow < a + v + 2), rows, 0.0) for v in (0, 2)]
                lhs = jnp.concatenate(lhs, axis=1).astype(jnp.bfloat16)
                four = jbuf[h, pl.ds(base + a, 4)].reshape(4 * blk, vox)
                total = total + jnp.dot(lhs, four, preferred_element_type=jnp.float32)
            calc_ref[h, pl.ds(base, GROUP), :] = total
        for u in range(GROUP):
            left, right = jbuf[0, base + u], jbuf[1, base + u]
            gram = nt_dot(jnp.concatenate([left, right], axis=1), diagonal_pair(left, right, zero))
            one, two = tb[base + u], tb[side_tiles + base + u]
            low_sum, high_sum = acc[one] + gram, acc[two] + gram
            pltpu.store(acc.at[one], low_sum, mask=low)
            pltpu.store(acc.at[two], high_sum, mask=high)
        return carry

    for c, part in enumerate(parts):
        part.wait()
        lax.fori_loop(c * groups, (c + 1) * groups, group, 0, unroll=GRAM_UNROLL)

    chunks = keep_ref.shape[0]
    pairs = keep_ref.shape[1] // half
    row = lax.broadcasted_iota(jnp.int32, (half, 2 * blk), 0)
    lane = lax.broadcasted_iota(jnp.int32, (half, 2 * blk), 1) % blk
    use_top = ((lane < half) & (row <= lane)) | ((lane >= half) & (lane - half <= row))
    frow = lax.broadcasted_iota(jnp.int32, (blk, 2 * blk), 0)
    flane = lax.broadcasted_iota(jnp.int32, (blk, 2 * blk), 1) % blk
    on_diag = frow == flane
    for part, ref in enumerate((send_ref, keep_ref)):
        def chunk(c, carry, part=1 - part, ref=ref):
            first = first_block(part, c, chunks, 2 * pairs)
            for p in range(pairs):
                one, two = acc[first + 2 * p], acc[first + 2 * p + 1]
                stay, cross = jnp.where(low, one, two), jnp.where(low, two, one)
                ref[c, p * half : (p + 1) * half, :] = jnp.where(use_top, stay[:half], stay[half:]) + pltpu.roll(
                    jnp.where(use_top, cross[:half], cross[half:]), blk, 1
                )
                lines = [jnp.sum(jnp.where(on_diag, v, 0.0), axis=0, keepdims=True) for v in (stay, cross)]
                diag_ref[part, c, p : p + 1, :] = lines[0] + pltpu.roll(lines[1], blk, 1)
            return carry

        lax.fori_loop(0, chunks, chunk, 0, unroll=PACK_UNROLL)


def grad_body(tb_ref, jbuf, calc_ref, obs_ref, mir_ref, diag_ref, keep_ref, send_ref, tg, mix):
    side_tiles, blk, vox = jbuf.shape[1:]
    tb_rows = tb_ref[...]
    back = vox - 1 - lax.broadcasted_iota(jnp.int32, (GROUP, vox), 1)
    up = GROUP - 1 - lax.broadcasted_iota(jnp.int32, (GROUP, vox), 0)
    lrow = lax.broadcasted_iota(jnp.int32, (2 * GROUP, 4 * blk), 0)
    lslot = lax.broadcasted_iota(jnp.int32, (2 * GROUP, 4 * blk), 1) // blk

    def group(g, mis):
        base = pl.multiple_of(g * GROUP, GROUP)
        rows = pl.ds(base, GROUP)
        resids = []
        for h in range(2):
            mirror = mir_ref[1 - h, pl.ds(pl.multiple_of(side_tiles - GROUP - base, GROUP), GROUP), :]
            mirror = gathered(gathered(mirror, back, 1), up, 0)
            resid = 0.5 * (obs_ref[h, rows, :] + mirror) - calc_ref[h, rows, :]
            mis = mis + resid * resid
            resids.append(resid)
        none = jnp.zeros_like(resids[0])
        lhs = jnp.concatenate(
            [jnp.concatenate([resids[0], none], axis=0), jnp.concatenate([none, resids[1]], axis=0)], axis=1
        ).astype(jnp.bfloat16)
        lines = jnp.zeros((2 * GROUP, 4 * blk), jnp.float32)
        for a in range(0, GROUP, 4):
            four = [jbuf[h, pl.ds(base + a, 4)].reshape(4 * blk, vox) for h in range(2)]
            out = nt_dot(lhs, jnp.concatenate(four, axis=1))
            lines = jnp.where((lrow & 7) == a + lslot, out, lines)
        tg[pl.ds(base, GROUP), :] = lines[:GROUP]
        tg[pl.ds(pl.multiple_of(side_tiles + base, GROUP), GROUP), :] = lines[GROUP:]
        return mis

    mis = lax.fori_loop(0, side_tiles // GROUP, group, jnp.zeros((GROUP, vox), jnp.float32), unroll=GRAD_UNROLL)

    chunks = keep_ref.shape[0]
    pairs = diag_ref.shape[2]
    total = jnp.sum(mis, axis=0, keepdims=True)
    rest = jnp.zeros((EXTRA - 2 * pairs - 1, vox), jnp.float32)
    block = lax.broadcasted_iota(jnp.int32, (NB, 2 * side_tiles), 0)
    own = jnp.dot(
        (block == tb_rows).astype(jnp.float32),
        tg[...],
        precision=lax.Precision.HIGHEST,
        preferred_element_type=jnp.float32,
    )
    own = own[:, : 2 * blk] + own[:, 2 * blk :]
    high = lax.broadcasted_iota(jnp.int32, own.shape, 1) >= blk
    odd = (lax.broadcasted_iota(jnp.int32, own.shape, 0) % 2) == 1
    mix[...] = jnp.where(odd == high, own + pltpu.roll(own, blk, 1), 0.0)
    for part, ref in enumerate((keep_ref, send_ref)):
        def chunk(c, carry, part=part, ref=ref):
            first = first_block(part, c, chunks, 2 * pairs)
            rows = [mix[pl.ds(first + 2 * p, 1), :] + mix[pl.ds(first + 2 * p + 1, 1), :] for p in range(pairs)]
            ref[c] = jnp.concatenate(rows + [diag_ref[part, c], total, rest], axis=0)
            return carry

        lax.fori_loop(0, chunks, chunk, 0, unroll=PACK_UNROLL)


def solve_body(damp, a_ref, b_ref, out_ref, mis_ref):
    x = a_ref[0] + b_ref[0]
    width = x.shape[1]
    blk = width // 2
    half = blk // 2
    tall = blk // 8
    pairs = (x.shape[0] - EXTRA) // half
    ext = x[pairs * half :]
    mis_ref[...] = jnp.broadcast_to(jnp.sum(ext[2 * pairs : 2 * pairs + 1], axis=1, keepdims=True), mis_ref.shape)
    row = lax.broadcasted_iota(jnp.int32, (half, width), 0)
    lane = lax.broadcasted_iota(jnp.int32, (half, width), 1)
    inner = lane % blk
    frow = lax.broadcasted_iota(jnp.int32, (blk, width), 0)
    flane = lax.broadcasted_iota(jnp.int32, (blk, width), 1)
    eye = frow == flane % blk
    scale = damp[0]
    mats = []
    rights = []
    diags = []
    for p in range(pairs):
        t = x[p * half : (p + 1) * half]
        grad = ext[p : p + 1]
        diag = ext[pairs + p : pairs + p + 1]
        tt = jnp.concatenate([t, jnp.zeros((width - half, width), jnp.float32)], axis=0).T
        mt = jnp.where(lane < blk, tt[:half], pltpu.roll(tt[blk : blk + half], blk, 1))
        bt = jnp.where(lane < blk, tt[half:blk], pltpu.roll(tt[blk + half :], blk, 1))
        top = jnp.where(
            inner < half,
            jnp.where(row <= inner, t, mt),
            jnp.where(inner - half <= row, t, pltpu.roll(mt, half, 1)),
        )
        bot = jnp.where(
            inner < half,
            jnp.where(row > inner, t, bt),
            jnp.where(inner - half > row, t, pltpu.roll(bt, half, 1)),
        )
        full = jnp.concatenate([top, bot], axis=0)
        full = jnp.where(eye, (diag + scale * diag) + 1.0, full)
        cols = jnp.where(eye, jnp.broadcast_to(grad, (blk, width)), 0.0)
        right = jnp.where(
            flane < blk,
            jnp.sum(jnp.where(flane < blk, cols, 0.0), axis=1, keepdims=True),
            jnp.sum(jnp.where(flane < blk, 0.0, cols), axis=1, keepdims=True),
        )
        mats.append([full[8 * i : 8 * i + 8] for i in range(tall)])
        rights.append([right[8 * i : 8 * i + 8] for i in range(tall)])
        diags.append(diag)
    sub = lax.broadcasted_iota(jnp.int32, (8, width), 0)
    lanes = lax.broadcasted_iota(jnp.int32, (8, width), 1)
    side = lanes - lanes % blk
    for k in range(0, blk, 8):
        own = k // 8
        for m, right in zip(mats, rights):
            cols = [[gathered(m[i], side + (k + j), 1) for i in range(tall)] for j in range(8)]
            held = [m] if k else [m, right]
            done = [part[own] for part in held]
            local = [col[own] for col in cols]
            for j in range(8):
                inverse = 1.0 / jnp.broadcast_to(local[j][j : j + 1], (8, width))

                def eliminate(part):
                    prow = jnp.broadcast_to(part[j : j + 1], (8, width)) * inverse
                    return jnp.where(sub == j, prow, part - local[j] * prow)

                local[j + 1 :] = [eliminate(part) for part in local[j + 1 :]]
                done = [eliminate(part) for part in done]
            for part, final in zip(held, done):
                prows = [jnp.broadcast_to(final[j : j + 1], (8, width)) for j in range(8)]
                for i in range(tall):
                    if i == own:
                        part[i] = final
                    else:
                        for j in range(8):
                            part[i] = part[i] - cols[j][i] * prows[j]
            if k == 0:
                m[:] = [jnp.where(lanes == side, right[i], m[i]) for i in range(tall)]
    lines = []
    for m, diag in zip(mats, diags):
        line = jnp.zeros((8, width), jnp.float32)
        for i in range(tall):
            line = line + jnp.where(eye[8 * i : 8 * i + 8], gathered(m[i], side, 1), 0.0)
        line = jnp.sum(line, axis=0, keepdims=True) * jnp.sqrt(diag)
        lines += [line, pltpu.roll(line, blk, 1)]
    out = jnp.concatenate(lines, axis=0)
    for c in range(out_ref.shape[0]):
        out_ref[c] = out


def fast(*args):
    return fast_inner(*args)


def fast_inner(observed, jacobian, tile_block, params, damping):
    ngx, ngy = lax.axis_size("gx"), lax.axis_size("gy")
    tiles, blk, vox = jacobian.shape
    per = NB // (ngx * ngy)
    half = blk // 2
    pairs = per // 2
    rows = pairs * half
    moved = flipped(observed, ("gx", "gy"), ngx * ngy)
    bits = ngx.bit_length() - 1
    side_tiles = tiles // 2
    local = lambda value: pltpu.with_memory_space_constraint(value, pltpu.VMEM)
    limit = pltpu.CompilerParams(vmem_limit_bytes=VMEM_LIMIT)
    halved = lambda value: value.reshape(2, side_tiles, *value.shape[1:])
    payload = pltpu.VMEM((ngx, rows, vox), jnp.float32)
    extra = pltpu.VMEM((ngx, EXTRA, vox), jnp.float32)
    smem = pl.BlockSpec(memory_space=pltpu.SMEM)
    vmem = pl.BlockSpec(memory_space=pltpu.VMEM)
    hbm = pl.BlockSpec(memory_space=pl.ANY)
    far = lambda value: pltpu.with_memory_space_constraint(value, pltpu.HBM)
    calc, keep, send, diag, staged = pl.pallas_call(
        gram_body,
        out_shape=(
            pltpu.VMEM((2, side_tiles, vox), jnp.float32),
            payload,
            payload,
            pltpu.VMEM((2, ngx, pairs, vox), jnp.float32),
            pltpu.VMEM((2, side_tiles, blk, vox), jnp.bfloat16),
        ),
        in_specs=[smem, hbm, vmem],
        out_specs=(vmem, vmem, vmem, vmem, vmem),
        scratch_shapes=[
            pltpu.VMEM((NB, blk, 2 * blk), jnp.float32),
            pltpu.VMEM((NB, 2 * blk), jnp.float32),
            pltpu.SemaphoreType.DMA((J_PARTS,)),
        ],
        compiler_params=limit,
        name="gram",
    )(far(tile_block), far(halved(jacobian)), far(params.T))
    other = xored(send, "gy", 1)
    got = plane(keep + other)
    keep, send = pl.pallas_call(
        grad_body,
        out_shape=(extra, extra),
        in_specs=[vmem] * 6,
        out_specs=(vmem, vmem),
        scratch_shapes=[pltpu.VMEM((tiles, 4 * blk), jnp.float32), pltpu.VMEM((NB, vox), jnp.float32)],
        compiler_params=limit,
        name="grad",
    )(tile_block[None], local(staged), local(calc), halved(observed), local(halved(moved)), local(diag))
    other = xored(send, "gy", 1)
    both = keep + other
    rest = plane(both)
    both = jnp.concatenate([got, rest], axis=1)
    mine, got = both, jnp.zeros_like(both)
    for s in range(PLANE.bit_length() - 1, bits):
        n = both.shape[0] // 2
        mine, got = both[:n], xored(both[n:], "gx", 1 << s)
        both = mine + got
    step, misfit = pl.pallas_call(
        solve_body,
        out_shape=(jax.ShapeDtypeStruct((ngx, per, vox), jnp.float32), jax.ShapeDtypeStruct((8, vox), jnp.float32)),
        in_specs=[smem, vmem, vmem],
        out_specs=(vmem, vmem),
        compiler_params=limit,
        name="solve",
    )(damping, local(mine), local(got))
    every = lax.all_to_all(step, "gx", 0, 0)
    return every.reshape(ngx * per, vox)[:, :blk], misfit[0, 0] / (tiles * ngx * ngy * vox)


def solve_blocks(system, rhs):
    size = system.shape[1]
    augmented = jnp.concatenate([system, rhs[:, :, None]], axis=2)
    augmented = jnp.transpose(augmented, (1, 2, 0))
    row_ids = jnp.arange(size, dtype=jnp.int32)

    def eliminate(step, current):
        column = step.astype(jnp.int32)
        pivot_row = lax.dynamic_index_in_dim(current, column, 0, keepdims=False)
        pivot = lax.dynamic_index_in_dim(pivot_row, column, 0, keepdims=False)
        pivot_row = pivot_row / pivot[None, :]
        factors = lax.dynamic_index_in_dim(current, column, 1, keepdims=False)
        updated = current - factors[:, None, :] * pivot_row[None, :, :]
        is_pivot = (row_ids == column)[:, None, None]
        return jnp.where(is_pivot, pivot_row[None, :, :], updated)

    final = lax.fori_loop(0, size, eliminate, augmented)
    return jnp.transpose(final[:, size, :], (1, 0))


def general(observed, jacobian, tile_block, params, damping):
    ngx, ngy = lax.axis_size("gx"), lax.axis_size("gy")
    moved = flipped(observed, ("gx", "gy"), ngx * ngy)[::-1, ::-1]
    block_ids = jnp.arange(NB, dtype=jnp.int32)
    onehot = (tile_block[:, None] == block_ids[None, :]).astype(jnp.float32)
    tile_params = jnp.dot(onehot, params, precision=lax.Precision.HIGHEST).astype(jnp.bfloat16)
    calc = jnp.einsum("tpv,tp->tv", jacobian, tile_params, preferred_element_type=jnp.float32)
    resid = 0.5 * (observed + moved) - calc
    local_misfit = jnp.sum(resid * resid)
    resid_b = resid.astype(jnp.bfloat16)
    tile_grad = jnp.einsum("tpv,tv->tp", jacobian, resid_b, preferred_element_type=jnp.float32)
    tile_gram = jnp.einsum("tpv,tqv->tpq", jacobian, jacobian, preferred_element_type=jnp.float32)
    gram = jnp.einsum("tb,tpq->bpq", onehot, tile_gram, precision=lax.Precision.HIGHEST)
    grad = jnp.dot(onehot.T, tile_grad, precision=lax.Precision.HIGHEST)
    owned = NB // ngy
    gram, grad, total = lax.psum((gram, grad, local_misfit), ("gx", "gy"))
    first = lax.axis_index("gy") * owned
    gram = lax.dynamic_slice_in_dim(gram, first, owned, 0)
    grad = lax.dynamic_slice_in_dim(grad, first, owned, 0)
    diagonal = jnp.diagonal(gram, axis1=1, axis2=2)
    eye = jnp.eye(gram.shape[1], dtype=jnp.float32)
    system = gram + damping[0] * diagonal[:, :, None] * eye[None] + eye[None]
    delta = solve_blocks(system, grad)
    return delta * jnp.sqrt(diagonal), total / (observed.size * ngx * ngy)


def solution(mesh):
    ngx, ngy = mesh.shape["gx"], mesh.shape["gy"]
    quick = ngy == 2 and ngx > PLANE and ngx & (ngx - 1) == 0 and NB % (2 * ngx * ngy) == 0
    return jax.shard_map(
        fast if quick else general,
        mesh=mesh,
        in_specs=(P(("gx", "gy"), None), P(("gx", "gy"), None, None), P(("gx", "gy")), P(), P()),
        out_specs=(P("gy", None), P()),
        check_vma=False,
    )
```

```python
import jax
import jax.numpy as jnp
from jax import lax
from jax.experimental import pallas as pl
from jax.experimental.pallas import tpu as pltpu
from jax.sharding import PartitionSpec as P

NB = 128
J_PARTS = 4
GROUP = 8
GRAM_UNROLL = 4
GRAD_UNROLL = 16
PACK_UNROLL = 4
VMEM_LIMIT = 20 << 20
EXTRA = 8
PLANE = 4


def flipped(value, axes, size):
    return lax.ppermute(value, axes, [(i, size - 1 - i) for i in range(size)])


def xored(value, axis, bit):
    return lax.ppermute(value, axis, [(i, i ^ bit) for i in range(lax.axis_size(axis))])


def plane(value):
    parts = value.reshape(PLANE, value.shape[0] // PLANE, *value.shape[1:])
    total = parts[0]
    for k in range(1, PLANE):
        total = total + xored(parts[k], "gx", k)
    return total


def nt_dot(a, b):
    return lax.dot_general(a, b, (((1,), (1,)), ((), ())), preferred_element_type=jnp.float32)


def gathered(value, index, axis):
    return jnp.take_along_axis(value, index, axis=axis, mode="promise_in_bounds")


def owner_of(c, chunks):
    line = chunks // PLANE
    bits = line.bit_length() - 1
    far = c % line
    swapped = sum(((far >> (bits - 1 - s)) & 1) << s for s in range(bits))
    return (c // line + PLANE * swapped) ^ lax.axis_index("gx")


def first_block(part, c, chunks, per):
    side = lax.axis_index("gy")
    return per * ((side if part == 0 else 1 - side) * chunks + owner_of(c, chunks))


def copies(j_ref, jbuf, sems):
    count = sems.shape[0]
    size = jbuf.shape[1] // count
    parts = []
    for c in range(count):
        rows = pl.ds(c * size, size)
        parts.append(pltpu.make_async_copy(j_ref.at[:, rows], jbuf.at[:, rows], sems.at[c]))
        parts[-1].start()
    return parts, size // GROUP


def diagonal_pair(left, right, zero):
    return jnp.concatenate(
        [jnp.concatenate([left, zero], axis=1), jnp.concatenate([zero, right], axis=1)], axis=0
    )


def gram_body(tb, j_ref, par_ref, calc_ref, keep_ref, send_ref, diag_ref, jbuf, acc, par, sems):
    parts, groups = copies(j_ref, jbuf, sems)
    side_tiles, blk, vox = jbuf.shape[1:]
    half = blk // 2
    acc[...] = jnp.zeros_like(acc)
    par[...] = jnp.concatenate([par_ref[...], par_ref[...]], axis=0).T.astype(jnp.bfloat16).astype(jnp.float32)
    zero = jnp.zeros((blk, vox), jnp.bfloat16)
    low = lax.broadcasted_iota(jnp.int32, (blk, 2 * blk), 1) < blk
    high = jnp.logical_not(low)
    grow = lax.broadcasted_iota(jnp.int32, (GROUP, 2 * blk), 0)
    gside = (lax.broadcasted_iota(jnp.int32, (GROUP, 2 * blk), 1) >= blk).astype(jnp.int32)
    slot = grow - (grow & 1) + gside
    fits = grow == slot

    def group(g, carry):
        base = pl.multiple_of(g * GROUP, GROUP)
        for h in range(2):
            rows = jnp.concatenate(
                [par[pl.ds(tb[h * side_tiles + base + u], 1), :] for u in range(GROUP)], axis=0
            )
            rows = jnp.where(fits, rows, 0.0)
            total = jnp.zeros((GROUP, vox), jnp.float32)
            for a in range(0, GROUP, 4):
                lhs = [jnp.where((grow >= a + v) & (grow < a + v + 2), rows, 0.0) for v in (0, 2)]
                lhs = jnp.concatenate(lhs, axis=1).astype(jnp.bfloat16)
                four = jbuf[h, pl.ds(base + a, 4)].reshape(4 * blk, vox)
                total = total + jnp.dot(lhs, four, preferred_element_type=jnp.float32)
            calc_ref[h, pl.ds(base, GROUP), :] = total
        for u in range(GROUP):
            left, right = jbuf[0, base + u], jbuf[1, base + u]
            gram = nt_dot(jnp.concatenate([left, right], axis=1), diagonal_pair(left, right, zero))
            one, two = tb[base + u], tb[side_tiles + base + u]
            low_sum, high_sum = acc[one] + gram, acc[two] + gram
            pltpu.store(acc.at[one], low_sum, mask=low)
            pltpu.store(acc.at[two], high_sum, mask=high)
        return carry

    for c, part in enumerate(parts):
        part.wait()
        lax.fori_loop(c * groups, (c + 1) * groups, group, 0, unroll=GRAM_UNROLL)

    chunks = keep_ref.shape[0]
    pairs = keep_ref.shape[1] // half
    row = lax.broadcasted_iota(jnp.int32, (half, 2 * blk), 0)
    lane = lax.broadcasted_iota(jnp.int32, (half, 2 * blk), 1) % blk
    use_top = ((lane < half) & (row <= lane)) | ((lane >= half) & (lane - half <= row))
    frow = lax.broadcasted_iota(jnp.int32, (blk, 2 * blk), 0)
    flane = lax.broadcasted_iota(jnp.int32, (blk, 2 * blk), 1) % blk
    on_diag = frow == flane
    for part, ref in enumerate((send_ref, keep_ref)):
        def chunk(c, carry, part=1 - part, ref=ref):
            first = first_block(part, c, chunks, 2 * pairs)
            for p in range(pairs):
                one, two = acc[first + 2 * p], acc[first + 2 * p + 1]
                stay, cross = jnp.where(low, one, two), jnp.where(low, two, one)
                ref[c, p * half : (p + 1) * half, :] = jnp.where(use_top, stay[:half], stay[half:]) + pltpu.roll(
                    jnp.where(use_top, cross[:half], cross[half:]), blk, 1
                )
                lines = [jnp.sum(jnp.where(on_diag, v, 0.0), axis=0, keepdims=True) for v in (stay, cross)]
                diag_ref[part, c, pairs + p : pairs + p + 1, :] = lines[0] + pltpu.roll(lines[1], blk, 1)
            return carry

        lax.fori_loop(0, chunks, chunk, 0, unroll=PACK_UNROLL)


def grad_body(tb_ref, jbuf, calc_ref, obs_ref, mir_ref, diag_ref, keep_ref, send_ref, tg, mix, paired):
    side_tiles, blk, vox = jbuf.shape[1:]
    tb_rows = tb_ref[...]
    back = vox - 1 - lax.broadcasted_iota(jnp.int32, (GROUP, vox), 1)
    up = GROUP - 1 - lax.broadcasted_iota(jnp.int32, (GROUP, vox), 0)
    lrow = lax.broadcasted_iota(jnp.int32, (2 * GROUP, 4 * blk), 0)
    lslot = lax.broadcasted_iota(jnp.int32, (2 * GROUP, 4 * blk), 1) // blk

    def group(g, mis):
        base = pl.multiple_of(g * GROUP, GROUP)
        rows = pl.ds(base, GROUP)
        resids = []
        for h in range(2):
            mirror = mir_ref[1 - h, pl.ds(pl.multiple_of(side_tiles - GROUP - base, GROUP), GROUP), :]
            mirror = gathered(gathered(mirror, back, 1), up, 0)
            resid = 0.5 * (obs_ref[h, rows, :] + mirror) - calc_ref[h, rows, :]
            mis = mis + resid * resid
            resids.append(resid)
        none = jnp.zeros_like(resids[0])
        lhs = jnp.concatenate(
            [jnp.concatenate([resids[0], none], axis=0), jnp.concatenate([none, resids[1]], axis=0)], axis=1
        ).astype(jnp.bfloat16)
        lines = jnp.zeros((2 * GROUP, 4 * blk), jnp.float32)
        for a in range(0, GROUP, 4):
            four = [jbuf[h, pl.ds(base + a, 4)].reshape(4 * blk, vox) for h in range(2)]
            out = nt_dot(lhs, jnp.concatenate(four, axis=1))
            lines = jnp.where((lrow & 7) == a + lslot, out, lines)
        lines = lines[:, : 2 * blk] + lines[:, 2 * blk :]
        tg[pl.ds(base, GROUP), :] = lines[:GROUP]
        tg[pl.ds(pl.multiple_of(side_tiles + base, GROUP), GROUP), :] = lines[GROUP:]
        return mis

    mis = lax.fori_loop(0, side_tiles // GROUP, group, jnp.zeros((GROUP, vox), jnp.float32), unroll=GRAD_UNROLL)

    chunks = keep_ref.shape[0]
    pairs = NB // (4 * chunks)
    total = jnp.sum(mis, axis=0, keepdims=True)
    sub = lax.broadcasted_iota(jnp.int32, (EXTRA, vox), 0)
    block = lax.broadcasted_iota(jnp.int32, (NB, 2 * side_tiles), 0)
    onehot = (block == tb_rows).astype(jnp.float32).astype(jnp.bfloat16)
    left_over = tg[...]
    own = jnp.zeros((NB, 2 * blk), jnp.float32)
    for _ in range(3):
        piece = left_over.astype(jnp.bfloat16)
        left_over = left_over - piece.astype(jnp.float32)
        own = own + jnp.dot(onehot, piece, preferred_element_type=jnp.float32)
    high = lax.broadcasted_iota(jnp.int32, own.shape, 1) >= blk
    odd = (lax.broadcasted_iota(jnp.int32, own.shape, 0) % 2) == 1
    mix[...] = jnp.where(odd == high, own + pltpu.roll(own, blk, 1), 0.0)
    paired[...] = mix[pl.ds(0, NB // 2, stride=2), :] + mix[pl.ds(1, NB // 2, stride=2), :]
    for part, ref in enumerate((keep_ref, send_ref)):
        for c in range(chunks):
            tile = jnp.where(sub == 2 * pairs, total, jnp.where(sub < 2 * pairs, diag_ref[part, c], 0.0))
            ref[c] = tile
            ref[c, :pairs, :] = paired[pl.ds(first_block(part, c, chunks, 2 * pairs) // 2, pairs), :]


def solve_body(damp, a_ref, b_ref, out_ref, mis_ref):
    x = a_ref[0] + b_ref[0]
    width = x.shape[1]
    blk = width // 2
    half = blk // 2
    tall = blk // 8
    pairs = (x.shape[0] - EXTRA) // half
    ext = x[pairs * half :]
    mis_ref[...] = jnp.broadcast_to(jnp.sum(ext[2 * pairs : 2 * pairs + 1], axis=1, keepdims=True), mis_ref.shape)
    row = lax.broadcasted_iota(jnp.int32, (half, width), 0)
    lane = lax.broadcasted_iota(jnp.int32, (half, width), 1)
    inner = lane % blk
    frow = lax.broadcasted_iota(jnp.int32, (blk, width), 0)
    flane = lax.broadcasted_iota(jnp.int32, (blk, width), 1)
    eye = frow == flane % blk
    scale = damp[0]
    mats = []
    rights = []
    diags = []
    for p in range(pairs):
        t = x[p * half : (p + 1) * half]
        grad = ext[p : p + 1]
        diag = ext[pairs + p : pairs + p + 1]
        tt = jnp.concatenate([t, jnp.zeros((width - half, width), jnp.float32)], axis=0).T
        mt = jnp.where(lane < blk, tt[:half], pltpu.roll(tt[blk : blk + half], blk, 1))
        bt = jnp.where(lane < blk, tt[half:blk], pltpu.roll(tt[blk + half :], blk, 1))
        top = jnp.where(
            inner < half,
            jnp.where(row <= inner, t, mt),
            jnp.where(inner - half <= row, t, pltpu.roll(mt, half, 1)),
        )
        bot = jnp.where(
            inner < half,
            jnp.where(row > inner, t, bt),
            jnp.where(inner - half > row, t, pltpu.roll(bt, half, 1)),
        )
        full = jnp.concatenate([top, bot], axis=0)
        full = jnp.where(eye, (diag + scale * diag) + 1.0, full)
        cols = jnp.where(eye, jnp.broadcast_to(grad, (blk, width)), 0.0)
        right = jnp.where(
            flane < blk,
            jnp.sum(jnp.where(flane < blk, cols, 0.0), axis=1, keepdims=True),
            jnp.sum(jnp.where(flane < blk, 0.0, cols), axis=1, keepdims=True),
        )
        mats.append([full[8 * i : 8 * i + 8] for i in range(tall)])
        rights.append([right[8 * i : 8 * i + 8] for i in range(tall)])
        diags.append(diag)
    sub = lax.broadcasted_iota(jnp.int32, (8, width), 0)
    lanes = lax.broadcasted_iota(jnp.int32, (8, width), 1)
    side = lanes - lanes % blk
    for k in range(0, blk, 8):
        own = k // 8
        for m, right in zip(mats, rights):
            cols = [[gathered(m[i], side + (k + j), 1) for i in range(tall)] for j in range(8)]
            held = [m] if k else [m, right]
            done = [part[own] for part in held]
            local = [col[own] for col in cols]
            for j in range(8):
                inverse = 1.0 / jnp.broadcast_to(local[j][j : j + 1], (8, width))

                def eliminate(part):
                    prow = jnp.broadcast_to(part[j : j + 1], (8, width)) * inverse
                    return jnp.where(sub == j, prow, part - local[j] * prow)

                local[j + 1 :] = [eliminate(part) for part in local[j + 1 :]]
                done = [eliminate(part) for part in done]
            for part, final in zip(held, done):
                prows = [jnp.broadcast_to(final[j : j + 1], (8, width)) for j in range(8)]
                for i in range(tall):
                    if i == own:
                        part[i] = final
                    else:
                        for j in range(8):
                            part[i] = part[i] - cols[j][i] * prows[j]
            if k == 0:
                m[:] = [jnp.where(lanes == side, right[i], m[i]) for i in range(tall)]
    lines = []
    for m, diag in zip(mats, diags):
        line = jnp.zeros((8, width), jnp.float32)
        for i in range(tall):
            line = line + jnp.where(eye[8 * i : 8 * i + 8], gathered(m[i], side, 1), 0.0)
        line = jnp.sum(line, axis=0, keepdims=True) * jnp.sqrt(diag)
        lines += [line, pltpu.roll(line, blk, 1)]
    out = jnp.concatenate(lines, axis=0)
    for c in range(out_ref.shape[0]):
        out_ref[c] = out


def fast(*args):
    return fast_inner(*args)


def fast_inner(observed, jacobian, tile_block, params, damping):
    ngx, ngy = lax.axis_size("gx"), lax.axis_size("gy")
    tiles, blk, vox = jacobian.shape
    per = NB // (ngx * ngy)
    half = blk // 2
    pairs = per // 2
    rows = pairs * half
    moved = flipped(observed, ("gx", "gy"), ngx * ngy)
    bits = ngx.bit_length() - 1
    side_tiles = tiles // 2
    local = lambda value: pltpu.with_memory_space_constraint(value, pltpu.VMEM)
    limit = pltpu.CompilerParams(vmem_limit_bytes=VMEM_LIMIT)
    halved = lambda value: value.reshape(2, side_tiles, *value.shape[1:])
    payload = pltpu.VMEM((ngx, rows, vox), jnp.float32)
    extra = pltpu.VMEM((ngx, EXTRA, vox), jnp.float32)
    smem = pl.BlockSpec(memory_space=pltpu.SMEM)
    vmem = pl.BlockSpec(memory_space=pltpu.VMEM)
    hbm = pl.BlockSpec(memory_space=pl.ANY)
    far = lambda value: pltpu.with_memory_space_constraint(value, pltpu.HBM)
    calc, keep, send, diag, staged = pl.pallas_call(
        gram_body,
        out_shape=(
            pltpu.VMEM((2, side_tiles, vox), jnp.float32),
            payload,
            payload,
            pltpu.VMEM((2, ngx, EXTRA, vox), jnp.float32),
            pltpu.VMEM((2, side_tiles, blk, vox), jnp.bfloat16),
        ),
        in_specs=[smem, hbm, vmem],
        out_specs=(vmem, vmem, vmem, vmem, vmem),
        scratch_shapes=[
            pltpu.VMEM((NB, blk, 2 * blk), jnp.float32),
            pltpu.VMEM((NB, 2 * blk), jnp.float32),
            pltpu.SemaphoreType.DMA((J_PARTS,)),
        ],
        compiler_params=limit,
        name="gram",
    )(far(tile_block), far(halved(jacobian)), far(params.T))
    other = xored(send, "gy", 1)
    got = plane(keep + other)
    keep, send = pl.pallas_call(
        grad_body,
        out_shape=(extra, extra),
        in_specs=[vmem] * 6,
        out_specs=(vmem, vmem),
        scratch_shapes=[
            pltpu.VMEM((tiles, 2 * blk), jnp.float32),
            pltpu.VMEM((NB, vox), jnp.float32),
            pltpu.VMEM((NB // 2, vox), jnp.float32),
        ],
        compiler_params=limit,
        name="grad",
    )(tile_block[None], local(staged), local(calc), halved(observed), local(halved(moved)), local(diag))
    other = xored(send, "gy", 1)
    both = keep + other
    rest = plane(both)
    both = jnp.concatenate([got, rest], axis=1)
    mine, got = both, jnp.zeros_like(both)
    for s in range(PLANE.bit_length() - 1, bits):
        n = both.shape[0] // 2
        mine, got = both[:n], xored(both[n:], "gx", 1 << s)
        both = mine + got
    step, misfit = pl.pallas_call(
        solve_body,
        out_shape=(jax.ShapeDtypeStruct((ngx, per, vox), jnp.float32), jax.ShapeDtypeStruct((8, vox), jnp.float32)),
        in_specs=[smem, vmem, vmem],
        out_specs=(vmem, vmem),
        compiler_params=limit,
        name="solve",
    )(damping, local(mine), local(got))
    every = lax.all_to_all(step, "gx", 0, 0)
    return every.reshape(ngx * per, vox)[:, :blk], misfit[0, 0] / (tiles * ngx * ngy * vox)


def solve_blocks(system, rhs):
    size = system.shape[1]
    augmented = jnp.concatenate([system, rhs[:, :, None]], axis=2)
    augmented = jnp.transpose(augmented, (1, 2, 0))
    row_ids = jnp.arange(size, dtype=jnp.int32)

    def eliminate(step, current):
        column = step.astype(jnp.int32)
        pivot_row = lax.dynamic_index_in_dim(current, column, 0, keepdims=False)
        pivot = lax.dynamic_index_in_dim(pivot_row, column, 0, keepdims=False)
        pivot_row = pivot_row / pivot[None, :]
        factors = lax.dynamic_index_in_dim(current, column, 1, keepdims=False)
        updated = current - factors[:, None, :] * pivot_row[None, :, :]
        is_pivot = (row_ids == column)[:, None, None]
        return jnp.where(is_pivot, pivot_row[None, :, :], updated)

    final = lax.fori_loop(0, size, eliminate, augmented)
    return jnp.transpose(final[:, size, :], (1, 0))


def general(observed, jacobian, tile_block, params, damping):
    ngx, ngy = lax.axis_size("gx"), lax.axis_size("gy")
    moved = flipped(observed, ("gx", "gy"), ngx * ngy)[::-1, ::-1]
    block_ids = jnp.arange(NB, dtype=jnp.int32)
    onehot = (tile_block[:, None] == block_ids[None, :]).astype(jnp.float32)
    tile_params = jnp.dot(onehot, params, precision=lax.Precision.HIGHEST).astype(jnp.bfloat16)
    calc = jnp.einsum("tpv,tp->tv", jacobian, tile_params, preferred_element_type=jnp.float32)
    resid = 0.5 * (observed + moved) - calc
    local_misfit = jnp.sum(resid * resid)
    resid_b = resid.astype(jnp.bfloat16)
    tile_grad = jnp.einsum("tpv,tv->tp", jacobian, resid_b, preferred_element_type=jnp.float32)
    tile_gram = jnp.einsum("tpv,tqv->tpq", jacobian, jacobian, preferred_element_type=jnp.float32)
    gram = jnp.einsum("tb,tpq->bpq", onehot, tile_gram, precision=lax.Precision.HIGHEST)
    grad = jnp.dot(onehot.T, tile_grad, precision=lax.Precision.HIGHEST)
    owned = NB // ngy
    gram, grad, total = lax.psum((gram, grad, local_misfit), ("gx", "gy"))
    first = lax.axis_index("gy") * owned
    gram = lax.dynamic_slice_in_dim(gram, first, owned, 0)
    grad = lax.dynamic_slice_in_dim(grad, first, owned, 0)
    diagonal = jnp.diagonal(gram, axis1=1, axis2=2)
    eye = jnp.eye(gram.shape[1], dtype=jnp.float32)
    system = gram + damping[0] * diagonal[:, :, None] * eye[None] + eye[None]
    delta = solve_blocks(system, grad)
    return delta * jnp.sqrt(diagonal), total / (observed.size * ngx * ngy)


def solution(mesh):
    ngx, ngy = mesh.shape["gx"], mesh.shape["gy"]
    quick = ngy == 2 and ngx > PLANE and ngx & (ngx - 1) == 0 and NB % (2 * ngx * ngy) == 0
    return jax.shard_map(
        fast if quick else general,
        mesh=mesh,
        in_specs=(P(("gx", "gy"), None), P(("gx", "gy"), None, None), P(("gx", "gy")), P(), P()),
        out_specs=(P("gy", None), P()),
        check_vma=False,
    )
```

```python
import jax
import jax.numpy as jnp
from jax import lax
from jax.experimental import pallas as pl
from jax.experimental.pallas import tpu as pltpu
from jax.sharding import PartitionSpec as P

NB = 128
J_PARTS = 4
GROUP = 8
GRAM_UNROLL = 4
GRAD_UNROLL = 16
PACK_UNROLL = 8
VMEM_LIMIT = 16 << 20
EXTRA = 8
PLANE = 4


def flipped(value, axes, size):
    return lax.ppermute(value, axes, [(i, size - 1 - i) for i in range(size)])


def xored(value, axis, bit):
    return lax.ppermute(value, axis, [(i, i ^ bit) for i in range(lax.axis_size(axis))])


def plane(value):
    parts = value.reshape(PLANE, value.shape[0] // PLANE, *value.shape[1:])
    total = parts[0]
    for k in range(1, PLANE):
        total = total + xored(parts[k], "gx", k)
    return total


def nt_dot(a, b):
    return lax.dot_general(a, b, (((1,), (1,)), ((), ())), preferred_element_type=jnp.float32)


def gathered(value, index, axis):
    return jnp.take_along_axis(value, index, axis=axis, mode="promise_in_bounds")


def owner_of(c, chunks):
    line = chunks // PLANE
    bits = line.bit_length() - 1
    far = c % line
    swapped = sum(((far >> (bits - 1 - s)) & 1) << s for s in range(bits))
    return (c // line + PLANE * swapped) ^ lax.axis_index("gx")


def first_block(part, c, chunks, per):
    side = lax.axis_index("gy")
    return per * ((side if part == 0 else 1 - side) * chunks + owner_of(c, chunks))


def copies(j_ref, jbuf, sems):
    count = sems.shape[0]
    size = jbuf.shape[1] // count
    parts = []
    for c in range(count):
        rows = pl.ds(c * size, size)
        parts.append(pltpu.make_async_copy(j_ref.at[:, rows], jbuf.at[:, rows], sems.at[c]))
        parts[-1].start()
    return parts, size // GROUP


def diagonal_pair(left, right, zero):
    return jnp.concatenate(
        [jnp.concatenate([left, zero], axis=1), jnp.concatenate([zero, right], axis=1)], axis=0
    )


def gram_body(tb, j_ref, par_ref, calc_ref, keep_ref, send_ref, diag_ref, jbuf, acc, par, sems):
    parts, groups = copies(j_ref, jbuf, sems)
    side_tiles, blk, vox = jbuf.shape[1:]
    half = blk // 2
    acc[...] = jnp.zeros_like(acc)
    par[:NB, :] = jnp.concatenate([par_ref[...], par_ref[...]], axis=0).T.astype(jnp.bfloat16).astype(jnp.float32)
    zero = jnp.zeros((blk, vox), jnp.bfloat16)
    low = lax.broadcasted_iota(jnp.int32, (blk, 2 * blk), 1) < blk
    high = jnp.logical_not(low)
    grow = lax.broadcasted_iota(jnp.int32, (GROUP, 2 * blk), 0)
    gside = (lax.broadcasted_iota(jnp.int32, (GROUP, 2 * blk), 1) >= blk).astype(jnp.int32)
    slot = grow - (grow & 1) + gside
    fits = grow == slot

    def group(g, carry):
        base = pl.multiple_of(g * GROUP, GROUP)
        for h in range(2):
            rows = jnp.concatenate(
                [par[pl.ds(tb[h * side_tiles + base + u], 1), :] for u in range(GROUP)], axis=0
            )
            rows = jnp.where(fits, rows, 0.0)
            total = jnp.zeros((GROUP, vox), jnp.float32)
            for a in range(0, GROUP, 4):
                lhs = [jnp.where((grow >= a + v) & (grow < a + v + 2), rows, 0.0) for v in (0, 2)]
                lhs = jnp.concatenate(lhs, axis=1).astype(jnp.bfloat16)
                four = jbuf[h, pl.ds(base + a, 4)].reshape(4 * blk, vox)
                total = total + jnp.dot(lhs, four, preferred_element_type=jnp.float32)
            calc_ref[h, pl.ds(base, GROUP), :] = total
        for u in range(GROUP):
            left, right = jbuf[0, base + u], jbuf[1, base + u]
            gram = nt_dot(jnp.concatenate([left, right], axis=1), diagonal_pair(left, right, zero))
            one, two = tb[base + u], tb[side_tiles + base + u]
            low_sum, high_sum = acc[one] + gram, acc[two] + gram
            pltpu.store(acc.at[one], low_sum, mask=low)
            pltpu.store(acc.at[two], high_sum, mask=high)
        return carry

    for c, part in enumerate(parts):
        part.wait()
        lax.fori_loop(c * groups, (c + 1) * groups, group, 0, unroll=GRAM_UNROLL)

    chunks = keep_ref.shape[0]
    pairs = keep_ref.shape[1] // half
    row = lax.broadcasted_iota(jnp.int32, (half, 2 * blk), 0)
    lane = lax.broadcasted_iota(jnp.int32, (half, 2 * blk), 1) % blk
    use_top = ((lane < half) & (row <= lane)) | ((lane >= half) & (lane - half <= row))
    frow = lax.broadcasted_iota(jnp.int32, (blk, 2 * blk), 0)
    flane = lax.broadcasted_iota(jnp.int32, (blk, 2 * blk), 1) % blk
    on_diag = frow == flane
    for part, ref in enumerate((send_ref, keep_ref)):
        def chunk(c, carry, part=1 - part, ref=ref):
            first = first_block(part, c, chunks, 2 * pairs)
            for p in range(pairs):
                one, two = acc[first + 2 * p], acc[first + 2 * p + 1]
                stay, cross = jnp.where(low, one, two), jnp.where(low, two, one)
                ref[c, p * half : (p + 1) * half, :] = jnp.where(use_top, stay[:half], stay[half:]) + pltpu.roll(
                    jnp.where(use_top, cross[:half], cross[half:]), blk, 1
                )
                lines = [jnp.sum(jnp.where(on_diag, v, 0.0), axis=0, keepdims=True) for v in (stay, cross)]
                diag_ref[part, c, pairs + p : pairs + p + 1, :] = lines[0] + pltpu.roll(lines[1], blk, 1)
            return carry

        lax.fori_loop(0, chunks, chunk, 0, unroll=PACK_UNROLL)


def grad_body(tb_ref, jbuf, calc_ref, obs_ref, mir_ref, diag_ref, keep_ref, send_ref, tg, mix, paired):
    side_tiles, blk, vox = jbuf.shape[1:]
    tb_rows = tb_ref[...]
    back = vox - 1 - lax.broadcasted_iota(jnp.int32, (GROUP, vox), 1)
    up = GROUP - 1 - lax.broadcasted_iota(jnp.int32, (GROUP, vox), 0)
    lrow = lax.broadcasted_iota(jnp.int32, (2 * GROUP, 4 * blk), 0)
    lslot = lax.broadcasted_iota(jnp.int32, (2 * GROUP, 4 * blk), 1) // blk

    def group(g, mis):
        base = pl.multiple_of(g * GROUP, GROUP)
        rows = pl.ds(base, GROUP)
        resids = []
        for h in range(2):
            mirror = mir_ref[1 - h, pl.ds(pl.multiple_of(side_tiles - GROUP - base, GROUP), GROUP), :]
            mirror = gathered(gathered(mirror, back, 1), up, 0)
            resid = 0.5 * (obs_ref[h, rows, :] + mirror) - calc_ref[h, rows, :]
            mis = mis + resid * resid
            resids.append(resid)
        none = jnp.zeros_like(resids[0])
        lhs = jnp.concatenate(
            [jnp.concatenate([resids[0], none], axis=0), jnp.concatenate([none, resids[1]], axis=0)], axis=1
        ).astype(jnp.bfloat16)
        lines = jnp.zeros((2 * GROUP, 4 * blk), jnp.float32)
        for a in range(0, GROUP, 4):
            four = [jbuf[h, pl.ds(base + a, 4)].reshape(4 * blk, vox) for h in range(2)]
            out = nt_dot(lhs, jnp.concatenate(four, axis=1))
            lines = jnp.where((lrow & 7) == a + lslot, out, lines)
        lines = lines[:, : 2 * blk] + lines[:, 2 * blk :]
        tg[pl.ds(base, GROUP), :] = lines[:GROUP]
        tg[pl.ds(pl.multiple_of(side_tiles + base, GROUP), GROUP), :] = lines[GROUP:]
        return mis

    mis = lax.fori_loop(0, side_tiles // GROUP, group, jnp.zeros((GROUP, vox), jnp.float32), unroll=GRAD_UNROLL)

    chunks = keep_ref.shape[0]
    pairs = NB // (4 * chunks)
    total = jnp.sum(mis, axis=0, keepdims=True)
    sub = lax.broadcasted_iota(jnp.int32, (EXTRA, vox), 0)
    block = lax.broadcasted_iota(jnp.int32, (NB, 2 * side_tiles), 0)
    onehot = (block == tb_rows).astype(jnp.float32).astype(jnp.bfloat16)
    left_over = tg[...]
    own = jnp.zeros((NB, 2 * blk), jnp.float32)
    for _ in range(3):
        piece = left_over.astype(jnp.bfloat16)
        left_over = left_over - piece.astype(jnp.float32)
        own = own + jnp.dot(onehot, piece, preferred_element_type=jnp.float32)
    high = lax.broadcasted_iota(jnp.int32, own.shape, 1) >= blk
    odd = (lax.broadcasted_iota(jnp.int32, own.shape, 0) % 2) == 1
    mix[:NB, :] = jnp.where(odd == high, own + pltpu.roll(own, blk, 1), 0.0)
    paired[: NB // 2, :] = mix[pl.ds(0, NB // 2, stride=2), :] + mix[pl.ds(1, NB // 2, stride=2), :]
    for part, ref in enumerate((keep_ref, send_ref)):
        for c in range(chunks):
            tile = jnp.where(sub == 2 * pairs, total, jnp.where(sub < 2 * pairs, diag_ref[part, c], 0.0))
            ref[c] = tile
            ref[c, :pairs, :] = paired[pl.ds(first_block(part, c, chunks, 2 * pairs) // 2, pairs), :]


def solve_body(damp, a_ref, b_ref, out_ref, mis_ref):
    x = a_ref[0] + b_ref[0]
    width = x.shape[1]
    blk = width // 2
    half = blk // 2
    tall = blk // 8
    pairs = (x.shape[0] - EXTRA) // half
    ext = x[pairs * half :]
    mis_ref[...] = jnp.broadcast_to(jnp.sum(ext[2 * pairs : 2 * pairs + 1], axis=1, keepdims=True), mis_ref.shape)
    row = lax.broadcasted_iota(jnp.int32, (half, width), 0)
    lane = lax.broadcasted_iota(jnp.int32, (half, width), 1)
    inner = lane % blk
    frow = lax.broadcasted_iota(jnp.int32, (blk, width), 0)
    flane = lax.broadcasted_iota(jnp.int32, (blk, width), 1)
    eye = frow == flane % blk
    scale = damp[0]
    mats = []
    rights = []
    diags = []
    for p in range(pairs):
        t = x[p * half : (p + 1) * half]
        grad = ext[p : p + 1]
        diag = ext[pairs + p : pairs + p + 1]
        tt = jnp.concatenate([t, jnp.zeros((width - half, width), jnp.float32)], axis=0).T
        mt = jnp.where(lane < blk, tt[:half], pltpu.roll(tt[blk : blk + half], blk, 1))
        bt = jnp.where(lane < blk, tt[half:blk], pltpu.roll(tt[blk + half :], blk, 1))
        top = jnp.where(
            inner < half,
            jnp.where(row <= inner, t, mt),
            jnp.where(inner - half <= row, t, pltpu.roll(mt, half, 1)),
        )
        bot = jnp.where(
            inner < half,
            jnp.where(row > inner, t, bt),
            jnp.where(inner - half > row, t, pltpu.roll(bt, half, 1)),
        )
        full = jnp.concatenate([top, bot], axis=0)
        full = jnp.where(eye, (diag + scale * diag) + 1.0, full)
        cols = jnp.where(eye, jnp.broadcast_to(grad, (blk, width)), 0.0)
        right = jnp.where(
            flane < blk,
            jnp.sum(jnp.where(flane < blk, cols, 0.0), axis=1, keepdims=True),
            jnp.sum(jnp.where(flane < blk, 0.0, cols), axis=1, keepdims=True),
        )
        mats.append([full[8 * i : 8 * i + 8] for i in range(tall)])
        rights.append([right[8 * i : 8 * i + 8] for i in range(tall)])
        diags.append(diag)
    sub = lax.broadcasted_iota(jnp.int32, (8, width), 0)
    lanes = lax.broadcasted_iota(jnp.int32, (8, width), 1)
    side = lanes - lanes % blk
    for k in range(0, blk, 8):
        own = k // 8
        for m, right in zip(mats, rights):
            cols = [[gathered(m[i], side + (k + j), 1) for i in range(tall)] for j in range(8)]
            held = [m] if k else [m, right]
            done = [part[own] for part in held]
            local = [col[own] for col in cols]
            for j in range(8):
                inverse = 1.0 / jnp.broadcast_to(local[j][j : j + 1], (8, width))

                def eliminate(part):
                    prow = jnp.broadcast_to(part[j : j + 1], (8, width)) * inverse
                    return jnp.where(sub == j, prow, part - local[j] * prow)

                local[j + 1 :] = [eliminate(part) for part in local[j + 1 :]]
                done = [eliminate(part) for part in done]
            for part, final in zip(held, done):
                prows = [jnp.broadcast_to(final[j : j + 1], (8, width)) for j in range(8)]
                for i in range(tall):
                    if i == own:
                        part[i] = final
                    else:
                        for j in range(8):
                            part[i] = part[i] - cols[j][i] * prows[j]
            if k == 0:
                m[:] = [jnp.where(lanes == side, right[i], m[i]) for i in range(tall)]
    lines = []
    for m, diag in zip(mats, diags):
        line = jnp.zeros((8, width), jnp.float32)
        for i in range(tall):
            line = line + jnp.where(eye[8 * i : 8 * i + 8], gathered(m[i], side, 1), 0.0)
        line = jnp.sum(line, axis=0, keepdims=True) * jnp.sqrt(diag)
        lines += [line, pltpu.roll(line, blk, 1)]
    out = jnp.concatenate(lines, axis=0)
    for c in range(out_ref.shape[0]):
        out_ref[c] = out


def fast(*args):
    return fast_inner(*args)


def fast_inner(observed, jacobian, tile_block, params, damping):
    ngx, ngy = lax.axis_size("gx"), lax.axis_size("gy")
    tiles, blk, vox = jacobian.shape
    per = NB // (ngx * ngy)
    half = blk // 2
    pairs = per // 2
    rows = pairs * half
    moved = flipped(observed, ("gx", "gy"), ngx * ngy)
    bits = ngx.bit_length() - 1
    side_tiles = tiles // 2
    local = lambda value: pltpu.with_memory_space_constraint(value, pltpu.VMEM)
    limit = pltpu.CompilerParams(vmem_limit_bytes=VMEM_LIMIT)
    halved = lambda value: value.reshape(2, side_tiles, *value.shape[1:])
    payload = pltpu.VMEM((ngx, rows, vox), jnp.float32)
    extra = pltpu.VMEM((ngx, EXTRA, vox), jnp.float32)
    smem = pl.BlockSpec(memory_space=pltpu.SMEM)
    vmem = pl.BlockSpec(memory_space=pltpu.VMEM)
    hbm = pl.BlockSpec(memory_space=pl.ANY)
    far = lambda value: pltpu.with_memory_space_constraint(value, pltpu.HBM)
    calc, keep, send, diag, staged = pl.pallas_call(
        gram_body,
        out_shape=(
            pltpu.VMEM((2, side_tiles, vox), jnp.float32),
            payload,
            payload,
            pltpu.VMEM((2, ngx, EXTRA, vox), jnp.float32),
            pltpu.VMEM((2, side_tiles, blk, vox), jnp.bfloat16),
        ),
        in_specs=[smem, hbm, vmem],
        out_specs=(vmem, vmem, vmem, vmem, vmem),
        scratch_shapes=[
            pltpu.VMEM((NB, blk, 2 * blk), jnp.float32),
            pltpu.VMEM((NB + GROUP, 2 * blk), jnp.float32),
            pltpu.SemaphoreType.DMA((J_PARTS,)),
        ],
        compiler_params=limit,
        name="gram",
    )(far(tile_block), far(halved(jacobian)), far(params.T))
    other = xored(send, "gy", 1)
    got = plane(keep + other)
    keep, send = pl.pallas_call(
        grad_body,
        out_shape=(extra, extra),
        in_specs=[vmem] * 6,
        out_specs=(vmem, vmem),
        scratch_shapes=[
            pltpu.VMEM((tiles, 2 * blk), jnp.float32),
            pltpu.VMEM((NB + GROUP, vox), jnp.float32),
            pltpu.VMEM((NB // 2 + GROUP, vox), jnp.float32),
        ],
        compiler_params=limit,
        name="grad",
    )(tile_block[None], local(staged), local(calc), halved(observed), local(halved(moved)), local(diag))
    other = xored(send, "gy", 1)
    both = keep + other
    rest = plane(both)
    both = jnp.concatenate([got, rest], axis=1)
    mine, got = both, jnp.zeros_like(both)
    for s in range(PLANE.bit_length() - 1, bits):
        n = both.shape[0] // 2
        mine, got = both[:n], xored(both[n:], "gx", 1 << s)
        both = mine + got
    step, misfit = pl.pallas_call(
        solve_body,
        out_shape=(jax.ShapeDtypeStruct((ngx, per, vox), jnp.float32), jax.ShapeDtypeStruct((8, vox), jnp.float32)),
        in_specs=[smem, vmem, vmem],
        out_specs=(vmem, vmem),
        compiler_params=limit,
        name="solve",
    )(damping, local(mine), local(got))
    every = lax.all_to_all(step, "gx", 0, 0)
    return every.reshape(ngx * per, vox)[:, :blk], misfit[0, 0] / (tiles * ngx * ngy * vox)


def solve_blocks(system, rhs):
    size = system.shape[1]
    augmented = jnp.concatenate([system, rhs[:, :, None]], axis=2)
    augmented = jnp.transpose(augmented, (1, 2, 0))
    row_ids = jnp.arange(size, dtype=jnp.int32)

    def eliminate(step, current):
        column = step.astype(jnp.int32)
        pivot_row = lax.dynamic_index_in_dim(current, column, 0, keepdims=False)
        pivot = lax.dynamic_index_in_dim(pivot_row, column, 0, keepdims=False)
        pivot_row = pivot_row / pivot[None, :]
        factors = lax.dynamic_index_in_dim(current, column, 1, keepdims=False)
        updated = current - factors[:, None, :] * pivot_row[None, :, :]
        is_pivot = (row_ids == column)[:, None, None]
        return jnp.where(is_pivot, pivot_row[None, :, :], updated)

    final = lax.fori_loop(0, size, eliminate, augmented)
    return jnp.transpose(final[:, size, :], (1, 0))


def general(observed, jacobian, tile_block, params, damping):
    ngx, ngy = lax.axis_size("gx"), lax.axis_size("gy")
    moved = flipped(observed, ("gx", "gy"), ngx * ngy)[::-1, ::-1]
    block_ids = jnp.arange(NB, dtype=jnp.int32)
    onehot = (tile_block[:, None] == block_ids[None, :]).astype(jnp.float32)
    tile_params = jnp.dot(onehot, params, precision=lax.Precision.HIGHEST).astype(jnp.bfloat16)
    calc = jnp.einsum("tpv,tp->tv", jacobian, tile_params, preferred_element_type=jnp.float32)
    resid = 0.5 * (observed + moved) - calc
    local_misfit = jnp.sum(resid * resid)
    resid_b = resid.astype(jnp.bfloat16)
    tile_grad = jnp.einsum("tpv,tv->tp", jacobian, resid_b, preferred_element_type=jnp.float32)
    tile_gram = jnp.einsum("tpv,tqv->tpq", jacobian, jacobian, preferred_element_type=jnp.float32)
    gram = jnp.einsum("tb,tpq->bpq", onehot, tile_gram, precision=lax.Precision.HIGHEST)
    grad = jnp.dot(onehot.T, tile_grad, precision=lax.Precision.HIGHEST)
    owned = NB // ngy
    gram, grad, total = lax.psum((gram, grad, local_misfit), ("gx", "gy"))
    first = lax.axis_index("gy") * owned
    gram = lax.dynamic_slice_in_dim(gram, first, owned, 0)
    grad = lax.dynamic_slice_in_dim(grad, first, owned, 0)
    diagonal = jnp.diagonal(gram, axis1=1, axis2=2)
    eye = jnp.eye(gram.shape[1], dtype=jnp.float32)
    system = gram + damping[0] * diagonal[:, :, None] * eye[None] + eye[None]
    delta = solve_blocks(system, grad)
    return delta * jnp.sqrt(diagonal), total / (observed.size * ngx * ngy)


def solution(mesh):
    ngx, ngy = mesh.shape["gx"], mesh.shape["gy"]
    quick = ngy == 2 and ngx > PLANE and ngx & (ngx - 1) == 0 and NB % (2 * ngx * ngy) == 0
    return jax.shard_map(
        fast if quick else general,
        mesh=mesh,
        in_specs=(P(("gx", "gy"), None), P(("gx", "gy"), None, None), P(("gx", "gy")), P(), P()),
        out_specs=(P("gy", None), P()),
        check_vma=False,
    )
```
